256 devices in a mesh: leaf: 32 (over y, z), panel: 8 (over x, core).
Axes of the slice: x: 4, y: 4, z: 8, core: 2. Of those that a mesh axis runs over, the one named last changes fastest.
Arguments:
- child_front: float32 [32, 2, 8, 128, 2048], P('leaf', None, 'panel'), as said below
- parent_entries: float32 [32, 4, 8, 128, 512], P('leaf', None, 'panel'), as said below
- parent_of: int32 [32], replicated, may hold values from 0 to 31
- owner_slot: int32 [32], replicated, may hold values from 0 to 31, each once
- front_blocks: int32 [32], replicated, may hold values from 8 to 32, as said below
- block_lists: int32 [32, 8], replicated, may hold values from 0 to 31, as said below
Outputs:
- child_factor: float32 [32, 2, 8, 128, 1024], P('leaf', None, 'panel')
- parent_factor: float32 [32, 4, 8, 128, 512], P('leaf', None, 'panel')
The draws below stay inside these ranges and needn't reach their ends.
Inputs may be any that keep to these rules, and one draw needn't show every extreme that they name: `front_blocks`: each entry is a multiple of the panel axis size; the largest equals 32. `block_lists`: the entries of a row are distinct, each below front_blocks of the child's parent, and entry k leaves the same remainder as k when divided by the panel axis size. `child_front`: symmetric, with a positive definite leading block of every front. `parent_entries`: the leading 512 rows form a symmetric positive definite block.
All inputs are finite; a program needn't handle non-finite values.
Results may differ from the reference program's by a relative error of at most 0.00044.
Values may be sent and summed in bfloat16 or wider, within the bound.
No kernel may reach another device: no remote copies, remote signals or barrier semaphores. Data moves between devices by JAX's collectives and lax.ppermute only.
A program may use at most 128 MiB of HBM per device.

```python
import math
import jax
import jax.numpy as jnp
from jax import lax

BLK = 128
PANEL = 512
WC = 2048
PC = 1024
W2 = 4096
CBW = 1024
CBB = 8
W2B = 32
NCH = 32
NPAR = 32
N_PANEL = 8


shift_value = 0.25


def rough_noise(key, shape):
    first_key = jax.random.fold_in(key, 7)
    noise = jax.random.normal(first_key, shape, jnp.float32)
    return noise


def definite_one(key, order):
    factor_rows = rough_noise(key, (order, order))
    gram = jnp.dot(factor_rows, factor_rows.T, precision=lax.Precision.HIGHEST) * (1.0 / order)
    gram = (gram + gram.T) * 0.5
    return gram + shift_value * jnp.eye(order, dtype=jnp.float32)


def definite_many(key, count_in, order):
    keys = jax.random.split(key, count_in)
    return lax.map(lambda single: definite_one(single, order), keys)


def draw_child_front(key, part):
    whole = definite_many(jax.random.fold_in(key, 21), NCH, WC)
    return whole.reshape(NCH, WC // (BLK * N_PANEL), N_PANEL, BLK, WC)


def draw_parent_entries(key, part):
    base_key = jax.random.fold_in(key, 22)
    top = definite_many(jax.random.fold_in(base_key, 1), NPAR, PANEL)
    rest = rough_noise(jax.random.fold_in(base_key, 2), (NPAR, W2 - PANEL, PANEL)) * (1.0 / math.sqrt(PANEL))
    whole = jnp.concatenate([top, rest], axis=1)
    return whole.reshape(NPAR, W2 // (BLK * N_PANEL), N_PANEL, BLK, PANEL)


def tree_tables(key):
    first_key = jax.random.fold_in(key, 101)
    second_key = jax.random.fold_in(key, 102)
    third_key = jax.random.fold_in(key, 103)
    fourth_key = jax.random.fold_in(key, 104)
    first = jax.random.randint(first_key, (NCH,), 0, NPAR)
    second = jax.random.randint(second_key, (NCH,), 0, NPAR)
    parent = jnp.minimum(first, second)
    parent = jnp.where(jnp.arange(NCH) == NCH - 1, NPAR - 1, parent)
    classes = W2B // N_PANEL
    per_class = CBB // N_PANEL
    live_blocks = N_PANEL * jax.random.randint(third_key, (NPAR,), per_class, classes + 1)
    live_blocks = jnp.where(jnp.arange(NPAR) == NPAR - 1, W2B, live_blocks)
    available = live_blocks[parent] // N_PANEL
    candidate = jnp.arange(classes)[None, :, None]
    scores = jax.random.randint(fourth_key, (NCH, classes, N_PANEL), 0, 1 << 20) * classes + candidate
    scores = jnp.where(candidate < available[:, None, None], scores, scores + (1 << 20) * classes)
    forced = jnp.logical_and((jnp.arange(NCH) == NCH - 1)[:, None, None], candidate == classes - 1)
    scores = jnp.where(forced, -1, scores)
    chosen = jnp.argsort(scores, axis=1, stable=True)[:, :per_class, :]
    blocks = chosen * N_PANEL + jnp.arange(N_PANEL)[None, None, :]
    return (parent.astype(jnp.int32), live_blocks.astype(jnp.int32), blocks.reshape(NCH, CBB).astype(jnp.int32))


def draw_parent_of(key, part):
    return tree_tables(key)[0]


def draw_front_blocks(key, part):
    return tree_tables(key)[1]


def draw_block_lists(key, part):
    return tree_tables(key)[2]


def setup_inputs(seed: int = 0) -> dict:
    splits = jax.random.split(jax.random.key(seed), 7)
    child_front = draw_child_front(jax.random.fold_in(splits[6], 71), 0)
    parent_entries = draw_parent_entries(jax.random.fold_in(splits[6], 71), 0)
    parent_of = draw_parent_of(jax.random.fold_in(splits[6], 71), 0)
    owner_slot = jax.random.permutation(splits[3], NPAR).astype(jnp.int32)
    front_blocks = draw_front_blocks(jax.random.fold_in(splits[6], 71), 0)
    block_lists = draw_block_lists(jax.random.fold_in(splits[6], 71), 0)
    return {"child_front": child_front, "parent_entries": parent_entries, "parent_of": parent_of, "owner_slot": owner_slot, "front_blocks": front_blocks, "block_lists": block_lists}


def partial_factor(front_matrix):
    factors = []
    for first_col in range(0, PC, PANEL):
        trailing = first_col + PANEL
        column = front_matrix[:, first_col:trailing]
        pivot_block = jnp.linalg.cholesky(column[first_col:trailing])
        all_rows = jax.scipy.linalg.solve_triangular(pivot_block, column.T, lower=True).T
        row_ids = jnp.arange(WC, dtype=jnp.int32)
        all_rows = jnp.where(row_ids[:, None] >= first_col, all_rows, 0.0)
        update = jnp.dot(all_rows, all_rows[trailing:].T, precision=lax.Precision.HIGHEST)
        front_matrix = jnp.concatenate([front_matrix[:, :trailing], front_matrix[:, trailing:] - update], axis=1)
        factors.append(all_rows)
    return (jnp.concatenate(factors, axis=1), front_matrix[PC:, PC:].astype(jnp.bfloat16))

def parent_solve(front_matrix):
    pivot_block = jnp.linalg.cholesky(front_matrix[:PANEL])
    return jax.scipy.linalg.solve_triangular(pivot_block, front_matrix.T, lower=True).T

def reference(child_front, parent_entries, parent_of, owner_slot, front_blocks, block_lists):
    fronts = child_front.reshape(NCH, WC, WC)
    factors, contribution = lax.map(partial_factor, fronts)
    child_factor = factors.reshape(NCH, WC // (BLK * N_PANEL), N_PANEL, BLK, PC)
    slot_of_child = owner_slot[parent_of].astype(jnp.int32)
    live_slot = jnp.zeros((NPAR,), jnp.int32).at[owner_slot].set(front_blocks)
    entries = parent_entries.reshape(NPAR, W2, PANEL)
    row_block = (jnp.arange(W2, dtype=jnp.int32) // BLK).astype(jnp.int32)
    live_rows = row_block[None, :] < live_slot[:, None]
    assembled = jnp.where(live_rows[:, :, None], entries, 0.0)
    within = (jnp.arange(CBW, dtype=jnp.int32) % BLK).astype(jnp.int32)
    block_of = (jnp.arange(CBW, dtype=jnp.int32) // BLK).astype(jnp.int32)

    def add_child(summed, inputs):
        block_rows, block_map, slot = inputs
        positions = (block_map[block_of] * BLK + within).astype(jnp.int32)
        summed = summed.at[slot, positions[:, None], positions[None, :]].add(block_rows.astype(jnp.float32), mode='drop')
        return (summed, None)
    assembled, _ = lax.scan(add_child, assembled, (contribution, block_lists, slot_of_child))
    parent_factor = lax.map(parent_solve, assembled).reshape(NPAR, W2 // (BLK * N_PANEL), N_PANEL, BLK, PANEL)
    return (child_factor, parent_factor)
```

```python
import jax
import jax.numpy as jnp
from jax import lax
from jax.experimental import pallas as pl
from jax.experimental.pallas import tpu as pltpu
from jax.sharding import PartitionSpec as P

BLK = 128
PANEL = 512
WC = 2048
PC = 1024
CBB = 8
NB = PANEL // BLK
SUB = 8
F32 = jnp.float32
BF16 = jnp.bfloat16


def split(a):
    hi = a.astype(BF16)
    return hi, (a - hi.astype(F32)).astype(BF16)


def dot_nn(a, b):
    return lax.dot_general(a, b, (((1,), (0,)), ((), ())), preferred_element_type=F32)


def dot_nt(a, b):
    return lax.dot_general(a, b, (((1,), (1,)), ((), ())), preferred_element_type=F32)


def mm(dot, a, b):
    (ah, al), (bh, bl) = a, b
    return dot(ah, bh) + (dot(al, bh) + dot(ah, bl))


def lanes(v, j):
    return jnp.broadcast_to(v[:, j : j + 1], (SUB, BLK))


def sublanes(v, k):
    return jnp.broadcast_to(v[k : k + 1, :], (SUB, BLK))


def factor_block(block):
    groups = BLK // SUB
    rows = [block[SUB * i : SUB * (i + 1), :] for i in range(groups)]
    sub = lax.broadcasted_iota(jnp.int32, (SUB, BLK), 0)
    lane = lax.broadcasted_iota(jnp.int32, (SUB, BLK), 1)
    for g in range(groups):
        first = SUB * g
        rest = range(1, groups - g)
        inside = (lane >= first) & (lane < first + SUB)
        cols = [[lanes(rows[i], first + k) for i in range(g, groups)] for k in range(SUB)]
        head = rows[g]
        below = [jnp.where(inside, 0.0, rows[g + i]) for i in rest]
        scale = jnp.zeros((SUB, BLK), F32)
        weights = []
        pivots = []
        for k in range(SUB):
            pivot = sublanes(cols[k][0], k)
            inv_sqrt = lax.rsqrt(pivot)
            inv = 1.0 / pivot
            scale = jnp.where(sub == k, inv_sqrt, scale)
            weights.append([cols[k][i] * inv for i in rest])
            for l in range(k + 1, SUB):
                ratio = sublanes(cols[l][0], k) * inv
                for i in range(groups - g):
                    cols[l][i] = cols[l][i] - cols[k][i] * ratio
            row = jnp.where(lane == first + k, 1.0, sublanes(head, k))
            weight = jnp.where(sub > k, cols[k][0] * inv, 0.0)
            head = jnp.where((lane == first + k) & (sub > k), 0.0, head) - weight * row
            pivots.append(jnp.where((lane > first + k) & (lane < first + SUB), 0.0, row))
        for i in rest:
            acc = below[i - 1]
            for k in range(SUB):
                acc = acc - weights[k][i - 1] * pivots[k]
            rows[g + i] = acc
        rows[g] = jnp.where(lane == first + sub, 1.0, head) * scale
    return jnp.concatenate(rows, axis=0)


def invert_panel(work, inv_hi, inv_lo):
    row = lax.broadcasted_iota(jnp.int32, (BLK, BLK), 0)
    col = lax.broadcasted_iota(jnp.int32, (BLK, BLK), 1)
    lane_block = lax.broadcasted_iota(jnp.int32, (BLK, PANEL), 1) // BLK

    def step(b, carry):
        here = pl.ds(pl.multiple_of(b * BLK, BLK), BLK)
        inv = jnp.where(row >= col, factor_block(work[b, :, here]), 0.0)
        inv_parts = split(inv)
        across = mm(dot_nn, inv_parts, split(work[b]))
        across = jnp.where(lane_block == b, jnp.concatenate([inv] * NB, axis=1), across)
        across_parts = split(across)
        work[b] = across
        for i in range(1, NB):

            @pl.when(i > b)
            def _():
                below = split(mm(dot_nt, split(work[i, :, here]), inv_parts))
                kept = jnp.where(lane_block == b, 0.0, work[i])
                work[i] = kept - mm(dot_nn, below, across_parts)

        return carry

    lax.fori_loop(0, NB, step, 0)
    for i in range(NB):
        hi, lo = split(jnp.where(lane_block <= i, work[i], 0.0))
        inv_hi[i * BLK : (i + 1) * BLK, :] = hi
        inv_lo[i * BLK : (i + 1) * BLK, :] = lo


def first_kernel(pivot, inv_hi, inv_lo, work):
    for i in range(NB):
        work[i] = pivot[i]
    invert_panel(work, inv_hi, inv_lo)


def child_kernel(mid, own, inv0_hi, inv0_lo, low, factor, contribution, work, inv1_hi, inv1_lo, mid_hi, mid_lo, low_hi, low_lo):
    inv0 = (inv0_hi[...], inv0_lo[...])

    def mid_rows(i):
        return (mid_hi[i * PANEL : (i + 1) * PANEL, :], mid_lo[i * PANEL : (i + 1) * PANEL, :])

    for half in (1, 0):
        for i in range(NB // 2):
            at = half * NB + 2 * i
            rows = mid[at : at + 2, :, :PANEL].reshape(2 * BLK, PANEL)
            hi, lo = split(mm(dot_nt, split(rows), inv0))
            mid_hi[at * BLK : (at + 2) * BLK, :] = hi
            mid_lo[at * BLK : (at + 2) * BLK, :] = lo
    for i in range(NB):
        at = PANEL + i * BLK
        part = (mid_hi[at : at + BLK, :], mid_lo[at : at + BLK, :])
        work[i] = mid[NB + i, :, PANEL:] - mm(dot_nt, part, mid_rows(1))
    invert_panel(work, inv1_hi, inv1_lo)
    inv1 = (inv1_hi[...], inv1_lo[...])
    for i in range(NB):
        part = (mid_hi[i * BLK : (i + 1) * BLK, :], mid_lo[i * BLK : (i + 1) * BLK, :])
        rows = mid[i, :, PANEL:] - mm(dot_nt, part, mid_rows(1))
        hi, lo = split(mm(dot_nt, split(rows), inv1))
        low_hi[i * BLK : (i + 1) * BLK, :] = hi
        low_lo[i * BLK : (i + 1) * BLK, :] = lo
    for s in range(2):
        first = mm(dot_nt, split(own[s, :, :PANEL]), inv0)
        first_parts = split(first)
        rows = own[s, :, PANEL:PC] - mm(dot_nt, first_parts, mid_rows(1))
        second = mm(dot_nt, split(rows), inv1)
        factor[s, :, :PANEL] = first
        if s == 0:
            factor[s, :, PANEL:] = jnp.where(low[0] == 1, 0.0, second)
        else:
            factor[s, :, PANEL:] = second
            rest = own[s, :, PC : PC + PANEL] - mm(dot_nt, first_parts, mid_rows(0))
            rest = rest - mm(dot_nt, split(second), (low_hi[...], low_lo[...]))
            contribution[...] = rest.astype(BF16)


def assemble_kernel(at, parent_of, owner_slot, front_blocks, block_lists, entries, gathered, out, buf, sem):
    leaf = at[0]
    panel = at[1]

    def find(q, live):
        return jnp.where(owner_slot[q] == leaf, front_blocks[q], live)

    live = lax.fori_loop(0, owner_slot.shape[0], find, jnp.int32(0))
    for t in range(entries.shape[0]):
        alive = t * at[2] + panel < live
        out[t] = jnp.where(alive, entries[t], 0.0)

    def add(c, carry):
        @pl.when(owner_slot[parent_of[c]] == leaf)
        def _():
            copy = pltpu.make_async_copy(gathered.at[c], buf, sem)
            copy.start()
            copy.wait()
            t = block_lists[c, panel] // at[2]
            for k in range(NB):

                @pl.when(block_lists[c, k] == k)
                def _():
                    cols = slice(k * BLK, (k + 1) * BLK)
                    out[t, :, cols] = out[t, :, cols] + buf[:, cols].astype(F32)

        return carry

    lax.fori_loop(0, parent_of.shape[0], add, 0)


def parent_kernel(pivot, rows, factor, work, inv_hi, inv_lo):
    for i in range(NB):
        work[i] = pivot[i]
    invert_panel(work, inv_hi, inv_lo)
    inv = (inv_hi[...], inv_lo[...])
    for t in range(rows.shape[0]):
        factor[t] = mm(dot_nt, split(rows[t]), inv)


VMEM = pl.BlockSpec(memory_space=pltpu.VMEM)
SMEM = pl.BlockSpec(memory_space=pltpu.SMEM)
ANY = pl.BlockSpec(memory_space=pl.ANY)
PARAMS = pltpu.CompilerParams(vmem_limit_bytes=48 * 1024 * 1024)


def shape(*dims, dtype=F32):
    return jax.ShapeDtypeStruct(dims, dtype)


def gather_pivot(block):
    return lax.all_gather(block, "panel", axis=0, tiled=True)[:NB]


def exchange(contribution):
    return lax.all_gather(contribution[None], "leaf", axis=0, tiled=True)


def on_device(child_front, parent_entries, parent_of, owner_slot, front_blocks, block_lists):
    panel_count = lax.axis_size("panel")
    panel = lax.axis_index("panel")
    leaf = lax.axis_index("leaf")
    parent_slots = parent_entries.shape[1]
    own = child_front.reshape(2, BLK, WC)
    with jax.named_scope("pivot0"):
        pivot = gather_pivot(own[:1, :, :PANEL])
    with jax.named_scope("mid"):
        one = jnp.where(panel >= NB, own[0, :, :PC], own[1, :, :PC])
        mid = lax.all_gather(one[None], "panel", axis=0, tiled=True)
    inv_shapes = (shape(PANEL, PANEL, dtype=BF16), shape(PANEL, PANEL, dtype=BF16))
    work = pltpu.VMEM((NB, BLK, PANEL), F32)
    half = pltpu.VMEM((PANEL, PANEL), BF16)
    full = pltpu.VMEM((2 * PANEL, PANEL), BF16)
    inv0_hi, inv0_lo = pl.pallas_call(
        first_kernel,
        out_shape=inv_shapes,
        in_specs=[VMEM],
        out_specs=(VMEM, VMEM),
        scratch_shapes=[work],
        compiler_params=PARAMS,
        name="first_panel",
    )(pivot)
    low = (panel < NB).astype(jnp.int32).reshape(1)
    factor, contribution = pl.pallas_call(
        child_kernel,
        out_shape=(shape(2, BLK, PC), shape(BLK, PANEL, dtype=BF16)),
        in_specs=[VMEM, VMEM, VMEM, VMEM, SMEM],
        out_specs=(VMEM, VMEM),
        scratch_shapes=[work, half, half, full, full, half, half],
        compiler_params=PARAMS,
        name="child",
    )(mid, own, inv0_hi, inv0_lo, low)
    with jax.named_scope("leaf_exchange"):
        gathered = exchange(contribution)
    at = jnp.stack([leaf, panel, panel_count]).astype(jnp.int32)
    assembled = pl.pallas_call(
        assemble_kernel,
        out_shape=shape(parent_slots, BLK, PANEL),
        in_specs=[SMEM, SMEM, SMEM, SMEM, SMEM, VMEM, ANY],
        out_specs=VMEM,
        scratch_shapes=[pltpu.VMEM((BLK, PANEL), BF16), pltpu.SemaphoreType.DMA],
        compiler_params=PARAMS,
        name="assemble",
    )(at, parent_of, owner_slot, front_blocks, block_lists, parent_entries.reshape(parent_slots, BLK, PANEL), gathered)
    with jax.named_scope("pivot2"):
        stacked = gather_pivot(assembled[:1])
    parent_factor = pl.pallas_call(
        parent_kernel,
        out_shape=shape(parent_slots, BLK, PANEL),
        in_specs=[VMEM, VMEM],
        out_specs=VMEM,
        scratch_shapes=[work, half, half],
        compiler_params=PARAMS,
        name="parent",
    )(stacked, assembled)
    return (factor.reshape(child_front.shape[:-1] + (PC,)), parent_factor.reshape(parent_entries.shape))


def solution(mesh):
    front = P("leaf", None, "panel", None, None)
    return jax.shard_map(
        on_device,
        mesh=mesh,
        in_specs=(front, front, P(), P(), P(), P()),
        out_specs=(front, front),
        check_vma=False,
    )
```

```python
import functools

import jax
import jax.numpy as jnp
from jax import lax
from jax.experimental import pallas as pl
from jax.experimental.pallas import tpu as pltpu
from jax.sharding import PartitionSpec as P

BLK = 128
PANEL = 512
WC = 2048
PC = 1024
CBB = 8
NB = PANEL // BLK
SUB = 8
F32 = jnp.float32
BF16 = jnp.bfloat16


def split(a):
    hi = a.astype(BF16)
    return hi, (a - hi.astype(F32)).astype(BF16)


def dot_nn(a, b):
    return lax.dot_general(a, b, (((1,), (0,)), ((), ())), preferred_element_type=F32)


def dot_nt(a, b):
    return lax.dot_general(a, b, (((1,), (1,)), ((), ())), preferred_element_type=F32)


def mm(dot, a, b):
    (ah, al), (bh, bl) = a, b
    return dot(ah, bh) + (dot(al, bh) + dot(ah, bl))


def lanes(v, j):
    return jnp.broadcast_to(v[:, j : j + 1], (SUB, BLK))


def sublanes(v, k):
    return jnp.broadcast_to(v[k : k + 1, :], (SUB, BLK))


def factor_block(block):
    groups = BLK // SUB
    rows = [block[SUB * i : SUB * (i + 1), :] for i in range(groups)]
    sub = lax.broadcasted_iota(jnp.int32, (SUB, BLK), 0)
    lane = lax.broadcasted_iota(jnp.int32, (SUB, BLK), 1)
    for g in range(groups):
        first = SUB * g
        rest = range(1, groups - g)
        inside = (lane >= first) & (lane < first + SUB)
        cols = [[lanes(rows[i], first + k) for i in range(g, groups)] for k in range(SUB)]
        head = rows[g]
        below = [jnp.where(inside, 0.0, rows[g + i]) for i in rest]
        scale = jnp.zeros((SUB, BLK), F32)
        weights = []
        pivots = []
        for k in range(SUB):
            pivot = sublanes(cols[k][0], k)
            inv_sqrt = lax.rsqrt(pivot)
            inv = 1.0 / pivot
            scale = jnp.where(sub == k, inv_sqrt, scale)
            weights.append([cols[k][i] * inv for i in rest])
            for l in range(k + 1, SUB):
                ratio = sublanes(cols[l][0], k) * inv
                for i in range(groups - g):
                    cols[l][i] = cols[l][i] - cols[k][i] * ratio
            row = jnp.where(lane == first + k, 1.0, sublanes(head, k))
            weight = jnp.where(sub > k, cols[k][0] * inv, 0.0)
            head = jnp.where((lane == first + k) & (sub > k), 0.0, head) - weight * row
            pivots.append(jnp.where((lane > first + k) & (lane < first + SUB), 0.0, row))
        for i in rest:
            acc = below[i - 1]
            for k in range(SUB):
                acc = acc - weights[k][i - 1] * pivots[k]
            rows[g + i] = acc
        rows[g] = jnp.where(lane == first + sub, 1.0, head) * scale
    return jnp.concatenate(rows, axis=0)


def invert_panel(work, inv_parts, beside=None):
    row = lax.broadcasted_iota(jnp.int32, (BLK, BLK), 0)
    col = lax.broadcasted_iota(jnp.int32, (BLK, BLK), 1)
    lane_block = lax.broadcasted_iota(jnp.int32, (BLK, PANEL), 1) // BLK

    def step(b, carry):
        here = pl.ds(pl.multiple_of(b * BLK, BLK), BLK)
        if beside is not None:
            beside(b)
        inv = jnp.where(row >= col, factor_block(work[b, :, here]), 0.0)
        inv = split(inv) + (inv,)
        across = mm(dot_nn, inv[:2], split(work[b]))
        across = jnp.where(lane_block == b, jnp.concatenate([inv[2]] * NB, axis=1), across)
        across_parts = split(across)
        work[b] = across
        for i in range(1, NB):

            @pl.when(i > b)
            def _():
                below = split(mm(dot_nt, split(work[i, :, here]), inv[:2]))
                kept = jnp.where(lane_block == b, 0.0, work[i])
                work[i] = kept - mm(dot_nn, below, across_parts)

        return carry

    lax.fori_loop(0, NB, step, 0)
    for i in range(NB):
        hi, lo = split(jnp.where(lane_block <= i, work[i], 0.0))
        inv_parts[0, i * BLK : (i + 1) * BLK, :] = hi
        inv_parts[1, i * BLK : (i + 1) * BLK, :] = lo


def take_pivot(core, blocks, work):
    for i in range(NB):
        work[(i // 2) * 2 + (core[0] + i) % 2] = blocks[i][...]


def first_kernel(core, b0, b1, b2, b3, inv_out, work, inv, sem):
    take_pivot(core, (b0, b1, b2, b3), work)
    invert_panel(work, inv)
    copy = pltpu.make_async_copy(inv, inv_out, sem)
    copy.start()
    copy.wait()


def child_kernel(mid_any, own, inv0_any, low, factor, contribution, mid, inv0_parts, work, inv1_parts, mid_parts, low_parts, low_rows, own_parts, own_rows, sems):
    upper = pltpu.make_async_copy(mid_any.at[pl.ds(NB, NB)], mid.at[pl.ds(NB, NB)], sems.at[0])
    lower = pltpu.make_async_copy(mid_any.at[pl.ds(0, NB)], mid.at[pl.ds(0, NB)], sems.at[1])
    inverse = pltpu.make_async_copy(inv0_any, inv0_parts, sems.at[2])
    inverse.start()
    upper.start()
    lower.start()
    inverse.wait()
    upper.wait()
    inv0 = (inv0_parts[0], inv0_parts[1])
    for i in range(NB // 2):
        at = PANEL + 2 * i * BLK
        rows = mid[NB + 2 * i : NB + 2 * i + 2, :, :PANEL].reshape(2 * BLK, PANEL)
        hi, lo = split(mm(dot_nt, split(rows), inv0))
        mid_parts[0, at : at + 2 * BLK, :] = hi
        mid_parts[1, at : at + 2 * BLK, :] = lo
    above = (mid_parts[0, PANEL:, :], mid_parts[1, PANEL:, :])
    for i in range(NB):
        at = PANEL + i * BLK
        part = (mid_parts[0, at : at + BLK, :], mid_parts[1, at : at + BLK, :])
        work[i] = mid[NB + i, :, PANEL:] - mm(dot_nt, part, above)
    lower.wait()
    chunk = 2 * BLK // NB

    def beside(b):
        inv0 = (inv0_parts[0], inv0_parts[1])
        above = (mid_parts[0, PANEL:, :], mid_parts[1, PANEL:, :])
        at = pl.ds(pl.multiple_of(b * BLK, BLK), BLK)
        part = split(mm(dot_nt, split(mid[b, :, :PANEL]), inv0))
        mid_parts[0, at, :] = part[0]
        mid_parts[1, at, :] = part[1]
        low_rows[at, :] = mid[b, :, PANEL:] - mm(dot_nt, part, above)
        s = b // 2
        rows = pl.ds(pl.multiple_of((b % 2) * chunk, chunk), chunk)
        to = pl.ds(pl.multiple_of(b * chunk, chunk), chunk)
        first = mm(dot_nt, split(own[s, rows, :PANEL]), inv0)
        factor[s, rows, :PANEL] = first
        part = split(first)
        own_parts[0, to, :] = part[0]
        own_parts[1, to, :] = part[1]
        own_rows[to, :] = own[s, rows, PANEL:PC] - mm(dot_nt, part, above)

    invert_panel(work, inv1_parts, beside)
    inv1 = (inv1_parts[0], inv1_parts[1])
    second = mm(dot_nt, split(own_rows[BLK:, :]), inv1)
    factor[1, :, PANEL:] = second
    for i in range(NB // 2):
        rows = slice(2 * i * BLK, 2 * (i + 1) * BLK)
        hi, lo = split(mm(dot_nt, split(low_rows[rows, :]), inv1))
        low_parts[0, rows, :] = hi
        low_parts[1, rows, :] = lo
    below = (mid_parts[0, :PANEL, :], mid_parts[1, :PANEL, :])
    rest = own[1, :, PC : PC + PANEL] - mm(dot_nt, (own_parts[0, BLK:, :], own_parts[1, BLK:, :]), below)
    rest = rest - mm(dot_nt, split(second), (low_parts[0], low_parts[1]))
    contribution[...] = rest.astype(BF16)
    factor[0, :, PANEL:] = jnp.where(low[0] == 1, 0.0, mm(dot_nt, split(own_rows[:BLK, :]), inv1))


def pack_kernel(at, parent_of, owner_slot, row, *rest):
    (*outs, sem) = rest
    zs = row.shape[0]
    ys = len(outs) + 1
    y = at[0] // zs
    z = at[0] % zs

    def each(act):
        for s in range(1, ys):
            target = ((y + s) % ys) * zs + z

            def step(i, k):
                hit = owner_slot[parent_of[y * zs + i]] == target

                @pl.when(hit)
                def _():
                    act(pltpu.make_async_copy(row.at[i], outs[s - 1].at[k], sem))

                return k + hit.astype(jnp.int32)

            lax.fori_loop(0, zs, step, jnp.int32(0))

    each(lambda copy: copy.start())
    each(lambda copy: copy.wait())


def assemble_kernel(at, parent_of, owner_slot, front_blocks, block_lists, entries, row, *rest, packed=True):
    (*others, out, buf, sem) = rest
    leaf = at[0]
    panel = at[1]
    zs = row.shape[0]
    ys = len(others) + 1

    def find(q, live):
        return jnp.where(owner_slot[q] == leaf, front_blocks[q], live)

    live = lax.fori_loop(0, owner_slot.shape[0], find, jnp.int32(0))
    for t in range(entries.shape[0]):
        alive = t * at[2] + panel < live
        out[t] = jnp.where(alive, entries[t], 0.0)

    def add(c):
        t = block_lists[c, panel] // at[2]
        for k in range(NB):

            @pl.when(block_lists[c, k] == k)
            def _():
                cols = slice(k * BLK, (k + 1) * BLK)
                out[t, :, cols] = out[t, :, cols] + buf[:, cols].astype(F32)

    def fetch(source):
        copy = pltpu.make_async_copy(source, buf, sem)
        copy.start()
        copy.wait()

    for s in range(ys):
        y = (leaf // zs + ys - s) % ys

        def step(i, k):
            c = y * zs + i
            hit = owner_slot[parent_of[c]] == leaf

            @pl.when(hit)
            def _():
                fetch(row.at[i] if s == 0 else others[s - 1].at[k if packed else i])
                add(c)

            return k + hit.astype(jnp.int32)

        lax.fori_loop(0, zs, step, jnp.int32(0))


def parent_kernel(core, b0, b1, b2, b3, rows, factor, work, inv_parts):
    take_pivot(core, (b0, b1, b2, b3), work)
    invert_panel(work, inv_parts)
    inv = (inv_parts[0], inv_parts[1])
    for t in range(rows.shape[0]):
        factor[t] = mm(dot_nt, split(rows[t]), inv)


VMEM = pl.BlockSpec(memory_space=pltpu.VMEM)
SMEM = pl.BlockSpec(memory_space=pltpu.SMEM)
ANY = pl.BlockSpec(memory_space=pl.ANY)
HBM = pl.BlockSpec(memory_space=pltpu.HBM)
YS = 4
ZS = 8


def limit(mib):
    return pltpu.CompilerParams(vmem_limit_bytes=mib * 1024 * 1024)


def shape(*dims, dtype=F32):
    return jax.ShapeDtypeStruct(dims, dtype)


def chip_permute(x, pairs):
    return lax.ppermute(x, "panel", [(2 * a + c, 2 * b + c) for a, b in pairs for c in range(2)])


def gather_pivot(block, panel):
    chip = panel // 2
    near = chip_permute(block, ((0, 1), (1, 0)))
    next_ = chip_permute(block, ((0, 3), (1, 2)))
    far = chip_permute(block, ((0, 2), (1, 3)))
    first = jnp.where(chip == 0, block, jnp.where(chip == 1, near, jnp.where(chip == 2, far, next_)))
    second = jnp.where(chip == 1, block, jnp.where(chip == 0, near, jnp.where(chip == 2, next_, far)))
    swap = [(i, i ^ 1) for i in range(8)]
    return first, lax.ppermute(first, "panel", swap), second, lax.ppermute(second, "panel", swap)


def along_z(contribution):
    groups = [[y * ZS + z for z in range(ZS)] for y in range(YS)]
    return lax.all_gather(contribution[None], "leaf", axis=0, tiled=True, axis_index_groups=groups)


def add_children(depth, at, tables, entries, row):
    parent_of, owner_slot, front_blocks, block_lists = tables
    if depth < ZS:
        sends = pl.pallas_call(
            pack_kernel,
            out_shape=(shape(depth, BLK, PANEL, dtype=BF16),) * (YS - 1),
            in_specs=[SMEM, SMEM, SMEM, ANY],
            out_specs=(ANY,) * (YS - 1),
            scratch_shapes=[pltpu.SemaphoreType.DMA],
            name=f"pack{depth}",
        )(at, parent_of, owner_slot, row)
    else:
        sends = None
    others = []
    for s in range(1, YS):
        pairs = [(y * ZS + z, ((y + s) % YS) * ZS + z) for y in range(YS) for z in range(ZS)]
        others.append(lax.ppermute(row if sends is None else sends[s - 1], "leaf", pairs))
    return pl.pallas_call(
        functools.partial(assemble_kernel, packed=sends is not None),
        out_shape=shape(*entries.shape),
        in_specs=[SMEM, SMEM, SMEM, SMEM, SMEM, VMEM] + [ANY] * YS,
        out_specs=VMEM,
        scratch_shapes=[pltpu.VMEM((BLK, PANEL), BF16), pltpu.SemaphoreType.DMA],
        compiler_params=limit(8),
        name=f"assemble{depth}",
    )(at, parent_of, owner_slot, front_blocks, block_lists, entries, row, *others)


def on_device(child_front, parent_entries, parent_of, owner_slot, front_blocks, block_lists):
    panel_count = lax.axis_size("panel")
    panel = lax.axis_index("panel")
    leaf = lax.axis_index("leaf")
    parent_slots = parent_entries.shape[1]
    own = child_front.reshape(2, BLK, WC)
    with jax.named_scope("mid"):
        one = jnp.where(panel >= NB, own[0, :, :PC], own[1, :, :PC])
        mid = lax.all_gather(one[None], "panel", axis=0, tiled=True)
    with jax.named_scope("pivot0"):
        blocks = gather_pivot(own[0, :, :PANEL], panel)
    core = (panel % 2).astype(jnp.int32).reshape(1)
    work = pltpu.VMEM((NB, BLK, PANEL), F32)
    parts = pltpu.VMEM((2, PANEL, PANEL), BF16)
    inv0 = pl.pallas_call(
        first_kernel,
        out_shape=shape(2, PANEL, PANEL, dtype=BF16),
        in_specs=[SMEM, VMEM, VMEM, VMEM, VMEM],
        out_specs=HBM,
        scratch_shapes=[work, parts, pltpu.SemaphoreType.DMA],
        compiler_params=limit(12),
        name="first_panel",
    )(core, *blocks)
    low = (panel < NB).astype(jnp.int32).reshape(1)
    factor, contribution = pl.pallas_call(
        child_kernel,
        out_shape=(shape(2, BLK, PC), shape(BLK, PANEL, dtype=BF16)),
        in_specs=[HBM, VMEM, HBM, SMEM],
        out_specs=(VMEM, VMEM),
        scratch_shapes=[
            pltpu.VMEM((2 * NB, BLK, PC), F32),
            parts,
            work,
            parts,
            pltpu.VMEM((2, 2 * PANEL, PANEL), BF16),
            parts,
            pltpu.VMEM((PANEL, PANEL), F32),
            pltpu.VMEM((2, 2 * BLK, PANEL), BF16),
            pltpu.VMEM((2 * BLK, PANEL), F32),
            pltpu.SemaphoreType.DMA((3,)),
        ],
        compiler_params=limit(28),
        name="child",
    )(mid, own, inv0, low)
    slots = jnp.sum(jnp.where(parent_of[:, None] == jnp.arange(owner_slot.shape[0])[None, :], owner_slot[None, :], 0), axis=1)
    hits = (slots[:, None] == jnp.arange(YS * ZS)[None, :]).reshape(YS, ZS, YS, ZS)
    counts = jnp.sum(hits.astype(jnp.int32), axis=1)
    elsewhere = jnp.arange(YS)[:, None, None] != jnp.arange(YS)[None, :, None]
    most = jnp.max(jnp.where(elsewhere, counts, 0))
    at = jnp.stack([leaf, panel, panel_count]).astype(jnp.int32)
    with jax.named_scope("along_z"):
        row = along_z(contribution)
    tables = (parent_of, owner_slot, front_blocks, block_lists)
    depths = (2, 3, ZS)
    with jax.named_scope("along_y"):
        assembled = lax.switch(
            (most > 2).astype(jnp.int32) + (most > 3).astype(jnp.int32),
            [lambda e, r, d=d: add_children(d, at, tables, e, r) for d in depths],
            parent_entries.reshape(parent_slots, BLK, PANEL),
            row,
        )
    with jax.named_scope("pivot2"):
        blocks = gather_pivot(assembled[0], panel)
    parent_factor = pl.pallas_call(
        parent_kernel,
        out_shape=shape(parent_slots, BLK, PANEL),
        in_specs=[SMEM, VMEM, VMEM, VMEM, VMEM, VMEM],
        out_specs=VMEM,
        scratch_shapes=[work, parts],
        compiler_params=limit(12),
        name="parent",
    )(core, *blocks, assembled)
    return (factor.reshape(child_front.shape[:-1] + (PC,)), parent_factor.reshape(parent_entries.shape))


def solution(mesh):
    front = P("leaf", None, "panel", None, None)
    return jax.shard_map(
        on_device,
        mesh=mesh,
        in_specs=(front, front, P(), P(), P(), P()),
        out_specs=(front, front),
        check_vma=False,
    )
```

```python
import functools

import jax
import jax.numpy as jnp
from jax import lax
from jax.experimental import pallas as pl
from jax.experimental.pallas import tpu as pltpu
from jax.sharding import PartitionSpec as P

BLK = 128
PANEL = 512
WC = 2048
PC = 1024
CBB = 8
NB = PANEL // BLK
SUB = 8
F32 = jnp.float32
BF16 = jnp.bfloat16


def split(a):
    hi = a.astype(BF16)
    return hi, (a - hi.astype(F32)).astype(BF16)


def dot_nn(a, b):
    return lax.dot_general(a, b, (((1,), (0,)), ((), ())), preferred_element_type=F32)


def dot_nt(a, b):
    return lax.dot_general(a, b, (((1,), (1,)), ((), ())), preferred_element_type=F32)


def mm(dot, a, b):
    (ah, al), (bh, bl) = a, b
    return dot(ah, bh) + (dot(al, bh) + dot(ah, bl))


def lanes(v, j):
    return jnp.broadcast_to(v[:, j : j + 1], (SUB, BLK))


def sublanes(v, k):
    return jnp.broadcast_to(v[k : k + 1, :], (SUB, BLK))


def factor_block(block):
    groups = BLK // SUB
    rows = [block[SUB * i : SUB * (i + 1), :] for i in range(groups)]
    sub = lax.broadcasted_iota(jnp.int32, (SUB, BLK), 0)
    lane = lax.broadcasted_iota(jnp.int32, (SUB, BLK), 1)
    for g in range(groups):
        first = SUB * g
        rest = range(1, groups - g)
        inside = (lane >= first) & (lane < first + SUB)
        cols = [[lanes(rows[i], first + k) for i in range(g, groups)] for k in range(SUB)]
        head = rows[g]
        below = [jnp.where(inside, 0.0, rows[g + i]) for i in rest]
        scale = jnp.zeros((SUB, BLK), F32)
        weights = []
        pivots = []
        for k in range(SUB):
            pivot = sublanes(cols[k][0], k)
            inv_sqrt = lax.rsqrt(pivot)
            inv = 1.0 / pivot
            scale = jnp.where(sub == k, inv_sqrt, scale)
            weights.append([cols[k][i] * inv for i in rest])
            for l in range(k + 1, SUB):
                ratio = sublanes(cols[l][0], k) * inv
                for i in range(groups - g):
                    cols[l][i] = cols[l][i] - cols[k][i] * ratio
            row = jnp.where(lane == first + k, 1.0, sublanes(head, k))
            weight = jnp.where(sub > k, cols[k][0] * inv, 0.0)
            head = jnp.where((lane == first + k) & (sub > k), 0.0, head) - weight * row
            pivots.append(jnp.where((lane > first + k) & (lane < first + SUB), 0.0, row))
        for i in rest:
            acc = below[i - 1]
            for k in range(SUB):
                acc = acc - weights[k][i - 1] * pivots[k]
            rows[g + i] = acc
        rows[g] = jnp.where(lane == first + sub, 1.0, head) * scale
    return jnp.concatenate(rows, axis=0)


def invert_panel(work, inv_parts, beside=None):
    row = lax.broadcasted_iota(jnp.int32, (BLK, BLK), 0)
    col = lax.broadcasted_iota(jnp.int32, (BLK, BLK), 1)
    lane_block = lax.broadcasted_iota(jnp.int32, (BLK, PANEL), 1) // BLK

    def step(b, carry):
        here = pl.ds(pl.multiple_of(b * BLK, BLK), BLK)
        if beside is not None:
            beside(b)
        inv = jnp.where(row >= col, factor_block(work[b, :, here]), 0.0)
        inv = split(inv) + (inv,)
        across = mm(dot_nn, inv[:2], split(work[b]))
        across = jnp.where(lane_block == b, jnp.concatenate([inv[2]] * NB, axis=1), across)
        across_parts = split(across)
        work[b] = across
        for i in range(1, NB):

            @pl.when(i > b)
            def _():
                below = split(mm(dot_nt, split(work[i, :, here]), inv[:2]))
                kept = jnp.where(lane_block == b, 0.0, work[i])
                work[i] = kept - mm(dot_nn, below, across_parts)

        return carry

    lax.fori_loop(0, NB, step, 0)
    for i in range(NB):
        hi, lo = split(jnp.where(lane_block <= i, work[i], 0.0))
        inv_parts[0, i * BLK : (i + 1) * BLK, :] = hi
        inv_parts[1, i * BLK : (i + 1) * BLK, :] = lo


def take_pivot(at, blocks, work, sem):
    core = at[1] % 2

    for chip, own in enumerate(((0, 1), (1, 0), (3, 2), (2, 3))):

        @pl.when(at[1] // 2 == chip)
        def _():
            for i in range(2):
                for k in range(2):
                    pltpu.make_async_copy(blocks[4 * k + own[i]], work.at[2 * i + (core + k) % 2], sem).start()

    pltpu.make_async_copy(work, work, sem).wait()


def first_kernel(at, b0, b1, b2, b3, b4, b5, b6, b7, inv_out, work, inv, sem):
    take_pivot(at, (b0, b1, b2, b3, b4, b5, b6, b7), work, sem)
    invert_panel(work, inv)
    copy = pltpu.make_async_copy(inv, inv_out, sem)
    copy.start()
    copy.wait()


def child_kernel(mid_any, own, inv0_any, low, factor, contribution, mid, inv0_parts, work, inv1_parts, mid_parts, low_parts, low_rows, own_parts, own_rows, sems):
    upper = pltpu.make_async_copy(mid_any.at[pl.ds(NB, NB)], mid.at[pl.ds(NB, NB)], sems.at[0])
    lower = pltpu.make_async_copy(mid_any.at[pl.ds(0, NB)], mid.at[pl.ds(0, NB)], sems.at[1])
    inverse = pltpu.make_async_copy(inv0_any, inv0_parts, sems.at[2])
    inverse.start()
    upper.start()
    lower.start()
    inverse.wait()
    upper.wait()
    inv0 = (inv0_parts[0], inv0_parts[1])
    for i in range(NB // 2):
        at = PANEL + 2 * i * BLK
        rows = mid[NB + 2 * i : NB + 2 * i + 2, :, :PANEL].reshape(2 * BLK, PANEL)
        hi, lo = split(mm(dot_nt, split(rows), inv0))
        mid_parts[0, at : at + 2 * BLK, :] = hi
        mid_parts[1, at : at + 2 * BLK, :] = lo
    above = (mid_parts[0, PANEL:, :], mid_parts[1, PANEL:, :])
    for i in range(NB):
        at = PANEL + i * BLK
        part = (mid_parts[0, at : at + BLK, :], mid_parts[1, at : at + BLK, :])
        work[i] = mid[NB + i, :, PANEL:] - mm(dot_nt, part, above)
    lower.wait()
    chunk = 2 * BLK // NB

    def beside(b):
        inv0 = (inv0_parts[0], inv0_parts[1])
        above = (mid_parts[0, PANEL:, :], mid_parts[1, PANEL:, :])
        at = pl.ds(pl.multiple_of(b * BLK, BLK), BLK)
        part = split(mm(dot_nt, split(mid[b, :, :PANEL]), inv0))
        mid_parts[0, at, :] = part[0]
        mid_parts[1, at, :] = part[1]
        low_rows[at, :] = mid[b, :, PANEL:] - mm(dot_nt, part, above)
        s = b // 2
        rows = pl.ds(pl.multiple_of((b % 2) * chunk, chunk), chunk)
        to = pl.ds(pl.multiple_of(b * chunk, chunk), chunk)
        first = mm(dot_nt, split(own[s, rows, :PANEL]), inv0)
        factor[s, rows, :PANEL] = first
        part = split(first)
        own_parts[0, to, :] = part[0]
        own_parts[1, to, :] = part[1]
        own_rows[to, :] = own[s, rows, PANEL:PC] - mm(dot_nt, part, above)

    invert_panel(work, inv1_parts, beside)
    inv1 = (inv1_parts[0], inv1_parts[1])
    second = mm(dot_nt, split(own_rows[BLK:, :]), inv1)
    factor[1, :, PANEL:] = second
    for i in range(NB // 2):
        rows = slice(2 * i * BLK, 2 * (i + 1) * BLK)
        hi, lo = split(mm(dot_nt, split(low_rows[rows, :]), inv1))
        low_parts[0, rows, :] = hi
        low_parts[1, rows, :] = lo
    below = (mid_parts[0, :PANEL, :], mid_parts[1, :PANEL, :])
    rest = own[1, :, PC : PC + PANEL] - mm(dot_nt, (own_parts[0, BLK:, :], own_parts[1, BLK:, :]), below)
    rest = rest - mm(dot_nt, split(second), (low_parts[0], low_parts[1]))
    contribution[...] = rest.astype(BF16)
    factor[0, :, PANEL:] = jnp.where(low[0] == 1, 0.0, mm(dot_nt, split(own_rows[:BLK, :]), inv1))


def place_row(row, r):
    own, back1, on1, back2, on2, back3, on3, back4, on4 = row
    whole = slice(0, BLK)
    low, high = slice(0, BLK // 2), slice(BLK // 2, BLK)
    return (
        [(own, whole)],
        [(on1, whole)],
        [(on2, whole)],
        [(on3, whole)],
        [(back4, low), (on4, high)],
        [(back3, whole)],
        [(back2, whole)],
        [(back1, whole)],
    )[r]


def pack_kernel(at, parent_of, owner_slot, *rest):
    row, outs, sem = rest[:9], rest[9:-1], rest[-1]
    y = at[0] // ZS
    z = at[0] % ZS
    total = jnp.int32(0)
    counts = [jnp.int32(0)] * (YS - 1)
    for r in range(ZS):
        slot = owner_slot[parent_of[y * ZS + (z + r) % ZS]]
        for s in range(1, YS):
            hit = slot == ((y + s) % YS) * ZS + z
            k = counts[s - 1]

            @pl.when(hit)
            def _():
                for source, rows in place_row(row, r):
                    pltpu.make_async_copy(source, outs[s - 1].at[k, rows], sem).start()

            counts[s - 1] = k + hit.astype(jnp.int32)
            total = total + hit.astype(jnp.int32)

    def wait(i, carry):
        pltpu.make_async_copy(row[0], outs[0].at[0], sem).wait()
        return carry

    lax.fori_loop(0, total, wait, 0)


def assemble_kernel(at, parent_of, owner_slot, front_blocks, block_lists, entries, *rest):
    row, others, out, pivot, buf, who, sem = rest[:9], rest[9 : 9 + YS - 1], *rest[9 + YS - 1 :]
    leaf = at[0]
    panel = at[1]
    z = leaf % ZS
    total = jnp.int32(0)
    for s in range(YS):
        y = (leaf // ZS + YS - s) % YS
        k = jnp.int32(0)
        for r in range(ZS):
            c = y * ZS + (z + r) % ZS
            hit = owner_slot[parent_of[c]] == leaf

            @pl.when(hit)
            def _():
                who[total] = c
                sources = place_row(row, r) if s == 0 else [(others[s - 1].at[k], slice(0, BLK))]
                for source, rows in sources:
                    pltpu.make_async_copy(source, buf.at[total, rows], sem).start()

            k = k + hit.astype(jnp.int32)
            total = total + hit.astype(jnp.int32)

    def find(q, live):
        return jnp.where(owner_slot[q] == leaf, front_blocks[q], live)

    live = lax.fori_loop(0, owner_slot.shape[0], find, jnp.int32(0))
    for t in range(entries.shape[0]):
        alive = t * at[2] + panel < live
        out[t] = jnp.where(alive, entries[t], 0.0)

    def wait(i, carry):
        pltpu.make_async_copy(row[0], buf.at[0], sem).wait()
        return carry

    lax.fori_loop(0, total, wait, 0)

    def add(i, carry):
        c = who[i]
        t = block_lists[c, panel] // at[2]
        for k in range(NB):

            @pl.when(block_lists[c, k] == k)
            def _():
                cols = slice(k * BLK, (k + 1) * BLK)
                out[t, :, cols] = out[t, :, cols] + buf[i, :, cols].astype(F32)

        return carry

    lax.fori_loop(0, total, add, 0)
    pivot[...] = out[0]


def parent_kernel(at, b0, b1, b2, b3, b4, b5, b6, b7, rows, factor, work, inv_parts, sem):
    take_pivot(at, (b0, b1, b2, b3, b4, b5, b6, b7), work, sem)
    invert_panel(work, inv_parts)
    inv = (inv_parts[0], inv_parts[1])
    for t in range(rows.shape[0]):
        factor[t] = mm(dot_nt, split(rows[t]), inv)


VMEM = pl.BlockSpec(memory_space=pltpu.VMEM)
SMEM = pl.BlockSpec(memory_space=pltpu.SMEM)
ANY = pl.BlockSpec(memory_space=pl.ANY)
HBM = pl.BlockSpec(memory_space=pltpu.HBM)
YS = 4
ZS = 8


def limit(mib):
    return pltpu.CompilerParams(vmem_limit_bytes=mib * 1024 * 1024)


def shape(*dims, dtype=F32):
    return jax.ShapeDtypeStruct(dims, dtype)


def chip_permute(x, pairs):
    return lax.ppermute(x, "panel", [(2 * a + c, 2 * b + c) for a, b in pairs for c in range(2)])


def gather_pivot(block):
    near = chip_permute(block, ((0, 1), (1, 0)))
    next_ = chip_permute(block, ((0, 3), (1, 2)))
    far = chip_permute(block, ((0, 2), (1, 3)))
    blocks = (block, near, next_, far)
    return blocks + tuple(lax.ppermute(b, "panel", [(i, i ^ 1) for i in range(8)]) for b in blocks)


def z_permute(x, s):
    return lax.ppermute(x, "leaf", [(y * ZS + z, y * ZS + (z + s) % ZS) for y in range(YS) for z in range(ZS)])


def along_z(own):
    back1, on1 = z_permute(own, 1), z_permute(own, -1)
    back2, on2 = z_permute(own, 2), z_permute(own, -2)
    back3, on3 = z_permute(back1, 2), z_permute(on1, -2)
    back4, on4 = z_permute(back2[: BLK // 2], 2), z_permute(on2[BLK // 2 :], -2)
    return own, back1, on1, back2, on2, back3, on3, back4, on4


def add_children(depth, at, tables, entries, row):
    parent_of, owner_slot, front_blocks, block_lists = tables
    sends = pl.pallas_call(
        pack_kernel,
        out_shape=(shape(depth, BLK, PANEL, dtype=BF16),) * (YS - 1),
        in_specs=[SMEM, SMEM, SMEM] + [ANY] * 9,
        out_specs=(ANY,) * (YS - 1),
        scratch_shapes=[pltpu.SemaphoreType.DMA],
        name=f"pack{depth}",
    )(at, parent_of, owner_slot, *row)
    others = []
    for s in range(1, YS):
        pairs = [(y * ZS + z, ((y + s) % YS) * ZS + z) for y in range(YS) for z in range(ZS)]
        others.append(lax.ppermute(sends[s - 1], "leaf", pairs))
    return pl.pallas_call(
        assemble_kernel,
        out_shape=(shape(*entries.shape), shape(BLK, PANEL)),
        in_specs=[SMEM, SMEM, SMEM, SMEM, SMEM, VMEM] + [ANY] * (9 + YS - 1),
        out_specs=(VMEM, VMEM),
        scratch_shapes=[pltpu.VMEM((YS * ZS, BLK, PANEL), BF16), pltpu.SMEM((YS * ZS,), jnp.int32), pltpu.SemaphoreType.DMA],
        compiler_params=limit(12),
        name=f"assemble{depth}",
    )(at, parent_of, owner_slot, front_blocks, block_lists, entries, *row, *others)


def on_device(child_front, parent_entries, parent_of, owner_slot, front_blocks, block_lists):
    panel_count = lax.axis_size("panel")
    panel = lax.axis_index("panel")
    leaf = lax.axis_index("leaf")
    parent_slots = parent_entries.shape[1]
    own = child_front.reshape(2, BLK, WC)
    with jax.named_scope("mid"):
        one = jnp.where(panel >= NB, own[0, :, :PC], own[1, :, :PC])
        mid = lax.all_gather(one[None], "panel", axis=0, tiled=True)
    with jax.named_scope("pivot0"):
        blocks = gather_pivot(own[0, :, :PANEL])
    at = jnp.stack([leaf, panel, panel_count]).astype(jnp.int32)
    work = pltpu.VMEM((NB, BLK, PANEL), F32)
    parts = pltpu.VMEM((2, PANEL, PANEL), BF16)
    inv0 = pl.pallas_call(
        first_kernel,
        out_shape=shape(2, PANEL, PANEL, dtype=BF16),
        in_specs=[SMEM] + [ANY] * 8,
        out_specs=HBM,
        scratch_shapes=[work, parts, pltpu.SemaphoreType.DMA],
        compiler_params=limit(12),
        name="first_panel",
    )(at, *[pltpu.with_memory_space_constraint(b, pltpu.HBM) for b in blocks])
    low = (panel < NB).astype(jnp.int32).reshape(1)
    factor, contribution = pl.pallas_call(
        child_kernel,
        out_shape=(shape(2, BLK, PC), shape(BLK, PANEL, dtype=BF16)),
        in_specs=[HBM, VMEM, HBM, SMEM],
        out_specs=(VMEM, VMEM),
        scratch_shapes=[
            pltpu.VMEM((2 * NB, BLK, PC), F32),
            parts,
            work,
            parts,
            pltpu.VMEM((2, 2 * PANEL, PANEL), BF16),
            parts,
            pltpu.VMEM((PANEL, PANEL), F32),
            pltpu.VMEM((2, 2 * BLK, PANEL), BF16),
            pltpu.VMEM((2 * BLK, PANEL), F32),
            pltpu.SemaphoreType.DMA((3,)),
        ],
        compiler_params=limit(28),
        name="child",
    )(pltpu.with_memory_space_constraint(mid, pltpu.HBM), own, inv0, low)
    slots = jnp.sum(jnp.where(parent_of[:, None] == jnp.arange(owner_slot.shape[0])[None, :], owner_slot[None, :], 0), axis=1)
    hits = (slots[:, None] == jnp.arange(YS * ZS)[None, :]).reshape(YS, ZS, YS, ZS)
    counts = jnp.sum(hits.astype(jnp.int32), axis=1)
    elsewhere = jnp.arange(YS)[:, None, None] != jnp.arange(YS)[None, :, None]
    most = jnp.max(jnp.where(elsewhere, counts, 0))
    with jax.named_scope("along_z"):
        row = along_z(contribution)
    tables = (parent_of, owner_slot, front_blocks, block_lists)
    depths = (2, 3, ZS)
    with jax.named_scope("along_y"):
        assembled, pivot = lax.switch(
            (most > 2).astype(jnp.int32) + (most > 3).astype(jnp.int32),
            [lambda e, r, d=d: add_children(d, at, tables, e, r) for d in depths],
            parent_entries.reshape(parent_slots, BLK, PANEL),
            row,
        )
    with jax.named_scope("pivot2"):
        blocks = gather_pivot(pivot)
    parent_factor = pl.pallas_call(
        parent_kernel,
        out_shape=shape(parent_slots, BLK, PANEL),
        in_specs=[SMEM] + [ANY] * 8 + [VMEM],
        out_specs=VMEM,
        scratch_shapes=[work, parts, pltpu.SemaphoreType.DMA],
        compiler_params=limit(12),
        name="parent",
    )(at, *blocks, assembled)
    return (factor.reshape(child_front.shape[:-1] + (PC,)), parent_factor.reshape(parent_entries.shape))


def solution(mesh):
    front = P("leaf", None, "panel", None, None)
    return jax.shard_map(
        on_device,
        mesh=mesh,
        in_specs=(front, front, P(), P(), P(), P()),
        out_specs=(front, front),
        check_vma=False,
    )
```

```python
import functools

import jax
import jax.numpy as jnp
from jax import lax
from jax.experimental import pallas as pl
from jax.experimental.pallas import tpu as pltpu
from jax.sharding import PartitionSpec as P

BLK = 128
PANEL = 512
WC = 2048
PC = 1024
CBB = 8
NB = PANEL // BLK
SUB = 8
F32 = jnp.float32
BF16 = jnp.bfloat16


def split(a):
    hi = a.astype(BF16)
    return hi, (a - hi.astype(F32)).astype(BF16)


def dot_nn(a, b):
    return lax.dot_general(a, b, (((1,), (0,)), ((), ())), preferred_element_type=F32)


def dot_nt(a, b):
    return lax.dot_general(a, b, (((1,), (1,)), ((), ())), preferred_element_type=F32)


def mm(dot, a, b):
    (ah, al), (bh, bl) = a, b
    return dot(ah, bh) + (dot(al, bh) + dot(ah, bl))


def lanes(v, j):
    return jnp.broadcast_to(v[:, j : j + 1], (SUB, BLK))


def sublanes(v, k):
    return jnp.broadcast_to(v[k : k + 1, :], (SUB, BLK))


def total(terms):
    while len(terms) > 1:
        terms = [a + b for a, b in zip(terms[::2], terms[1::2])] + terms[len(terms) // 2 * 2 :]
    return terms[0]


def factor_block(block, one):
    count = BLK // SUB
    span = count // 2
    width = span * SUB
    sub = lax.broadcasted_iota(jnp.int32, (SUB, BLK), 0)
    lane = lax.broadcasted_iota(jnp.int32, (SUB, BLK), 1)
    rows = [block[SUB * i : SUB * (i + 1), :] for i in range(count)]
    out = [None] * count
    for half in range(2):
        base = half * span
        now = rows[base : base + span]
        cols = None
        for g in range(span):
            first = SUB * (base + g)
            inside = (lane >= first) & (lane < first + SUB)
            follows = g + 1 < span
            if cols is None:
                cols = [lanes(now[g], first + k) * one for k in range(SUB)]
            if follows:
                kept = [lanes(now[g + 1], first + k) for k in range(SUB)]
                after = [lanes(now[g + 1], first + SUB + k) for k in range(SUB)]
                weights = [w * one for w in kept]
            head = jnp.where(inside, jnp.where(lane == first + sub, 1.0, 0.0), now[g])
            done = jnp.zeros((SUB, BLK), F32)
            for k in range(SUB):
                across = [sublanes(cols[q], k) if q >= k else None for q in range(SUB)]
                inv = 1.0 / across[k]
                here = sub == k
                row = sublanes(head, k)
                for q in range(k + 1, SUB):
                    step = jnp.where(here, -across[q], cols[k] * across[q])
                    cols[q] = jnp.where(here, 0.0, cols[q]) - step * inv
                step = jnp.where(here, -row, cols[k] * row)
                done = jnp.where(here, row * lax.rsqrt(across[k]), done)
                head = jnp.where(here, 0.0, head) - step * inv
                if follows:
                    scaled = weights[k] * inv
                    for q in range(k + 1, SUB):
                        weights[q] = weights[q] - scaled * across[q]
                    for q in range(SUB):
                        after[q] = after[q] - scaled * sublanes(weights[k], q)
            out[base + g] = done
            if base + g == count - 1:
                break
            spread = [sublanes(head, k) for k in range(SUB)]
            others = list(range(g + 1, span)) + (list(range(g)) if half == 0 else [])
            for i in others:
                mult = kept if i == g + 1 else [lanes(now[i], first + k) for k in range(SUB)]
                now[i] = jnp.where(inside, 0.0, now[i]) - total([m * r for m, r in zip(mult, spread)])
            now[g] = head
            cols = after if follows else None
        if half == 0:
            below = jnp.concatenate(rows[span:], axis=0)
            solved = jnp.concatenate(now + [jnp.zeros((BLK - width, BLK), F32)], axis=0)
            left = lax.broadcasted_iota(jnp.int32, below.shape, 1) < width
            below = jnp.where(left, 0.0, below) - mm(dot_nn, split(below), split(solved))
            rows[span:] = [below[SUB * i : SUB * (i + 1), :] for i in range(count - span)]
    return jnp.concatenate(out, axis=0)


def invert_panel(at, work, inv_parts, beside=None):
    row = lax.broadcasted_iota(jnp.int32, (BLK, BLK), 0)
    col = lax.broadcasted_iota(jnp.int32, (BLK, BLK), 1)
    lane_block = lax.broadcasted_iota(jnp.int32, (BLK, PANEL), 1) // BLK
    one = jnp.full((SUB, BLK), 1.0, F32) * jnp.minimum(at[2], 1).astype(F32)

    def step(b, carry):
        here = pl.ds(pl.multiple_of(b * BLK, BLK), BLK)
        if beside is not None:
            beside(b)
        inv = jnp.where(row >= col, factor_block(work[b, :, here], one), 0.0)
        inv = split(inv) + (inv,)
        across = mm(dot_nn, inv[:2], split(work[b]))
        across = jnp.where(lane_block == b, jnp.concatenate([inv[2]] * NB, axis=1), across)
        across_parts = split(across)
        work[b] = across
        for i in range(1, NB):

            @pl.when(i > b)
            def _():
                below = split(mm(dot_nt, split(work[i, :, here]), inv[:2]))
                kept = jnp.where(lane_block == b, 0.0, work[i])
                work[i] = kept - mm(dot_nn, below, across_parts)

        return carry

    lax.fori_loop(0, NB, step, 0)
    for i in range(NB):
        hi, lo = split(jnp.where(lane_block <= i, work[i], 0.0))
        inv_parts[0, i * BLK : (i + 1) * BLK, :] = hi
        inv_parts[1, i * BLK : (i + 1) * BLK, :] = lo


def take_pivot(at, blocks, work, sem):
    core = at[1] % 2

    for chip, own in enumerate(((0, 1), (1, 0), (3, 2), (2, 3))):

        @pl.when(at[1] // 2 == chip)
        def _():
            for i in range(2):
                for k in range(2):
                    for part in range(4):
                        rows = slice(part * BLK // 4, (part + 1) * BLK // 4)
                        to = work.at[2 * i + (core + k) % 2, rows]
                        pltpu.make_async_copy(blocks[4 * k + own[i]].at[rows], to, sem).start()

    pltpu.make_async_copy(work, work, sem).wait()


def first_kernel(at, b0, b1, b2, b3, b4, b5, b6, b7, inv_out, work, inv, sem):
    take_pivot(at, (b0, b1, b2, b3, b4, b5, b6, b7), work, sem)
    invert_panel(at, work, inv)
    copy = pltpu.make_async_copy(inv, inv_out, sem)
    copy.start()
    copy.wait()


def child_kernel(at, mid, own, inv0_parts, factor, contribution, work, inv1_parts, mid_parts, low_parts, low_rows, own_parts, own_rows):
    inv0 = (inv0_parts[0], inv0_parts[1])
    for i in range(NB // 2):
        to = slice(PANEL + 2 * i * BLK, PANEL + 2 * (i + 1) * BLK)
        rows = mid[NB + 2 * i : NB + 2 * i + 2, :, :PANEL].reshape(2 * BLK, PANEL)
        hi, lo = split(mm(dot_nt, split(rows), inv0))
        mid_parts[0, to, :] = hi
        mid_parts[1, to, :] = lo
    above = (mid_parts[0, PANEL:, :], mid_parts[1, PANEL:, :])
    for i in range(NB):
        rows = slice(PANEL + i * BLK, PANEL + (i + 1) * BLK)
        part = (mid_parts[0, rows, :], mid_parts[1, rows, :])
        work[i] = mid[NB + i, :, PANEL:] - mm(dot_nt, part, above)
    chunk = 2 * BLK // NB

    def beside(b):
        inv0 = (inv0_parts[0], inv0_parts[1])
        above = (mid_parts[0, PANEL:, :], mid_parts[1, PANEL:, :])
        to = pl.ds(pl.multiple_of(b * BLK, BLK), BLK)
        part = split(mm(dot_nt, split(mid[b, :, :PANEL]), inv0))
        mid_parts[0, to, :] = part[0]
        mid_parts[1, to, :] = part[1]
        low_rows[to, :] = mid[b, :, PANEL:] - mm(dot_nt, part, above)
        s = b // 2
        rows = pl.ds(pl.multiple_of((b % 2) * chunk, chunk), chunk)
        to = pl.ds(pl.multiple_of(b * chunk, chunk), chunk)
        first = mm(dot_nt, split(own[s, rows, :PANEL]), inv0)
        factor[s, rows, :PANEL] = first
        part = split(first)
        own_parts[0, to, :] = part[0]
        own_parts[1, to, :] = part[1]
        own_rows[to, :] = own[s, rows, PANEL:PC] - mm(dot_nt, part, above)

    invert_panel(at, work, inv1_parts, beside)
    inv1 = (inv1_parts[0], inv1_parts[1])
    second = mm(dot_nt, split(own_rows[BLK:, :]), inv1)
    factor[1, :, PANEL:] = second
    for i in range(NB // 2):
        rows = slice(2 * i * BLK, 2 * (i + 1) * BLK)
        hi, lo = split(mm(dot_nt, split(low_rows[rows, :]), inv1))
        low_parts[0, rows, :] = hi
        low_parts[1, rows, :] = lo
    below = (mid_parts[0, :PANEL, :], mid_parts[1, :PANEL, :])
    rest = own[1, :, PC : PC + PANEL] - mm(dot_nt, (own_parts[0, BLK:, :], own_parts[1, BLK:, :]), below)
    rest = rest - mm(dot_nt, split(second), (low_parts[0], low_parts[1]))
    contribution[...] = rest.astype(BF16)
    factor[0, :, PANEL:] = jnp.where(at[1] < NB, 0.0, mm(dot_nt, split(own_rows[:BLK, :]), inv1))


def place_row(row, r):
    own, back1, on1, back2, on2, back3, on3, back4, on4 = row
    whole = slice(0, BLK)
    low, high = slice(0, BLK // 2), slice(BLK // 2, BLK)
    return (
        [(own, whole)],
        [(on1, whole)],
        [(on2, whole)],
        [(on3, whole)],
        [(back4, low), (on4, high)],
        [(back3, whole)],
        [(back2, whole)],
        [(back1, whole)],
    )[r]


def pack_kernel(at, parent_of, owner_slot, *rest):
    row, outs, sem = rest[:9], rest[9:-1], rest[-1]
    y = at[0] // ZS
    z = at[0] % ZS
    total = jnp.int32(0)
    counts = [jnp.int32(0)] * (YS - 1)
    for r in range(ZS):
        slot = owner_slot[parent_of[y * ZS + (z + r) % ZS]]
        for s in range(1, YS):
            hit = slot == ((y + s) % YS) * ZS + z
            k = counts[s - 1]

            @pl.when(hit)
            def _():
                for source, rows in place_row(row, r):
                    pltpu.make_async_copy(source, outs[s - 1].at[k, rows], sem).start()

            counts[s - 1] = k + hit.astype(jnp.int32)
            total = total + hit.astype(jnp.int32)

    def wait(i, carry):
        pltpu.make_async_copy(row[0], outs[0].at[0], sem).wait()
        return carry

    lax.fori_loop(0, total, wait, 0)


def assemble_kernel(at, parent_of, owner_slot, front_blocks, block_lists, entries, *rest):
    row, others, out, pivot, buf, who, sem = rest[:9], rest[9 : 9 + YS - 1], *rest[9 + YS - 1 :]
    leaf = at[0]
    panel = at[1]
    z = leaf % ZS
    total = jnp.int32(0)
    for s in range(YS):
        y = (leaf // ZS + YS - s) % YS
        k = jnp.int32(0)
        for r in range(ZS):
            c = y * ZS + (z + r) % ZS
            hit = owner_slot[parent_of[c]] == leaf

            @pl.when(hit)
            def _():
                who[total] = c
                sources = place_row(row, r) if s == 0 else [(others[s - 1].at[k], slice(0, BLK))]
                for source, rows in sources:
                    pltpu.make_async_copy(source, buf.at[total, rows], sem).start()

            k = k + hit.astype(jnp.int32)
            total = total + hit.astype(jnp.int32)

    def find(q, live):
        return jnp.where(owner_slot[q] == leaf, front_blocks[q], live)

    live = lax.fori_loop(0, owner_slot.shape[0], find, jnp.int32(0))
    for t in range(entries.shape[0]):
        alive = t * at[2] + panel < live
        out[t] = jnp.where(alive, entries[t], 0.0)

    def wait(i, carry):
        pltpu.make_async_copy(row[0], buf.at[0], sem).wait()
        return carry

    lax.fori_loop(0, total, wait, 0)

    def add(i, carry):
        c = who[i]
        t = block_lists[c, panel] // at[2]
        for k in range(NB):

            @pl.when(block_lists[c, k] == k)
            def _():
                cols = slice(k * BLK, (k + 1) * BLK)
                out[t, :, cols] = out[t, :, cols] + buf[i, :, cols].astype(F32)

        return carry

    lax.fori_loop(0, total, add, 0)
    pivot[...] = out[0]


def parent_kernel(at, b0, b1, b2, b3, b4, b5, b6, b7, rows, factor, work, inv_parts, sem):
    take_pivot(at, (b0, b1, b2, b3, b4, b5, b6, b7), work, sem)
    invert_panel(at, work, inv_parts)
    inv = (inv_parts[0], inv_parts[1])
    for t in range(rows.shape[0]):
        factor[t] = mm(dot_nt, split(rows[t]), inv)


VMEM = pl.BlockSpec(memory_space=pltpu.VMEM)
SMEM = pl.BlockSpec(memory_space=pltpu.SMEM)
ANY = pl.BlockSpec(memory_space=pl.ANY)
HBM = pl.BlockSpec(memory_space=pltpu.HBM)
YS = 4
ZS = 8


def limit(mib):
    return pltpu.CompilerParams(vmem_limit_bytes=mib * 1024 * 1024)


def shape(*dims, dtype=F32):
    return jax.ShapeDtypeStruct(dims, dtype)


def chip_permute(x, pairs):
    return lax.ppermute(x, "panel", [(2 * a + c, 2 * b + c) for a, b in pairs for c in range(2)])


def gather_pivot(block):
    near = chip_permute(block, ((0, 1), (1, 0)))
    next_ = chip_permute(block, ((0, 3), (1, 2)))
    far = chip_permute(block, ((0, 2), (1, 3)))
    blocks = (block, near, next_, far)
    return blocks + tuple(lax.ppermute(b, "panel", [(i, i ^ 1) for i in range(8)]) for b in blocks)


def z_permute(x, s):
    return lax.ppermute(x, "leaf", [(y * ZS + z, y * ZS + (z + s) % ZS) for y in range(YS) for z in range(ZS)])


def along_z(own):
    back1, on1 = z_permute(own, 1), z_permute(own, -1)
    back2, on2 = z_permute(own, 2), z_permute(own, -2)
    back3, on3 = z_permute(back1, 2), z_permute(on1, -2)
    back4, on4 = z_permute(back2[: BLK // 2], 2), z_permute(on2[BLK // 2 :], -2)
    return own, back1, on1, back2, on2, back3, on3, back4, on4


def add_children(depth, at, tables, entries, row):
    parent_of, owner_slot, front_blocks, block_lists = tables
    sends = pl.pallas_call(
        pack_kernel,
        out_shape=(shape(depth, BLK, PANEL, dtype=BF16),) * (YS - 1),
        in_specs=[SMEM, SMEM, SMEM] + [ANY] * 9,
        out_specs=(ANY,) * (YS - 1),
        scratch_shapes=[pltpu.SemaphoreType.DMA],
        name=f"pack{depth}",
    )(at, parent_of, owner_slot, *row)
    others = []
    for s in range(1, YS):
        pairs = [(y * ZS + z, ((y + s) % YS) * ZS + z) for y in range(YS) for z in range(ZS)]
        others.append(lax.ppermute(sends[s - 1], "leaf", pairs))
    return pl.pallas_call(
        assemble_kernel,
        out_shape=(shape(*entries.shape), shape(BLK, PANEL)),
        in_specs=[SMEM, SMEM, SMEM, SMEM, SMEM, VMEM] + [ANY] * (9 + YS - 1),
        out_specs=(VMEM, VMEM),
        scratch_shapes=[pltpu.VMEM((YS * ZS, BLK, PANEL), BF16), pltpu.SMEM((YS * ZS,), jnp.int32), pltpu.SemaphoreType.DMA],
        compiler_params=limit(12),
        name=f"assemble{depth}",
    )(at, parent_of, owner_slot, front_blocks, block_lists, entries, *row, *others)


def on_device(child_front, parent_entries, parent_of, owner_slot, front_blocks, block_lists):
    panel_count = lax.axis_size("panel")
    panel = lax.axis_index("panel")
    leaf = lax.axis_index("leaf")
    parent_slots = parent_entries.shape[1]
    own = child_front.reshape(2, BLK, WC)
    with jax.named_scope("mid"):
        one = jnp.where(panel >= NB, own[0, :, :PC], own[1, :, :PC])
        mid = lax.all_gather(one[None], "panel", axis=0, tiled=True)
    with jax.named_scope("pivot0"):
        blocks = gather_pivot(own[0, :, :PANEL])
    at = jnp.stack([leaf, panel, panel_count]).astype(jnp.int32)
    work = pltpu.VMEM((NB, BLK, PANEL), F32)
    parts = pltpu.VMEM((2, PANEL, PANEL), BF16)
    inv0 = pl.pallas_call(
        first_kernel,
        out_shape=shape(2, PANEL, PANEL, dtype=BF16),
        in_specs=[SMEM] + [ANY] * 8,
        out_specs=HBM,
        scratch_shapes=[work, parts, pltpu.SemaphoreType.DMA],
        compiler_params=limit(12),
        name="first_panel",
    )(at, *[pltpu.with_memory_space_constraint(b, pltpu.HBM) for b in blocks])
    factor, contribution = pl.pallas_call(
        child_kernel,
        out_shape=(shape(2, BLK, PC), shape(BLK, PANEL, dtype=BF16)),
        in_specs=[SMEM, VMEM, VMEM, VMEM],
        out_specs=(VMEM, VMEM),
        scratch_shapes=[
            work,
            parts,
            pltpu.VMEM((2, 2 * PANEL, PANEL), BF16),
            parts,
            pltpu.VMEM((PANEL, PANEL), F32),
            pltpu.VMEM((2, 2 * BLK, PANEL), BF16),
            pltpu.VMEM((2 * BLK, PANEL), F32),
        ],
        compiler_params=limit(28),
        name="child",
    )(at, mid, own, inv0)
    slots = jnp.sum(jnp.where(parent_of[:, None] == jnp.arange(owner_slot.shape[0])[None, :], owner_slot[None, :], 0), axis=1)
    hits = (slots[:, None] == jnp.arange(YS * ZS)[None, :]).reshape(YS, ZS, YS, ZS)
    counts = jnp.sum(hits.astype(jnp.int32), axis=1)
    elsewhere = jnp.arange(YS)[:, None, None] != jnp.arange(YS)[None, :, None]
    most = jnp.max(jnp.where(elsewhere, counts, 0))
    with jax.named_scope("along_z"):
        row = along_z(contribution)
    tables = (parent_of, owner_slot, front_blocks, block_lists)
    depths = (2, 3, ZS)
    with jax.named_scope("along_y"):
        assembled, pivot = lax.switch(
            (most > 2).astype(jnp.int32) + (most > 3).astype(jnp.int32),
            [lambda e, r, d=d: add_children(d, at, tables, e, r) for d in depths],
            parent_entries.reshape(parent_slots, BLK, PANEL),
            row,
        )
    with jax.named_scope("pivot2"):
        blocks = gather_pivot(pivot)
    parent_factor = pl.pallas_call(
        parent_kernel,
        out_shape=shape(parent_slots, BLK, PANEL),
        in_specs=[SMEM] + [ANY] * 8 + [VMEM],
        out_specs=VMEM,
        scratch_shapes=[work, parts, pltpu.SemaphoreType.DMA],
        compiler_params=limit(12),
        name="parent",
    )(at, *blocks, assembled)
    return (factor.reshape(child_front.shape[:-1] + (PC,)), parent_factor.reshape(parent_entries.shape))


def solution(mesh):
    front = P("leaf", None, "panel", None, None)
    return jax.shard_map(
        on_device,
        mesh=mesh,
        in_specs=(front, front, P(), P(), P(), P()),
        out_specs=(front, front),
        check_vma=False,
    )
```

```python
import functools

import jax
import jax.numpy as jnp
from jax import lax
from jax.experimental import pallas as pl
from jax.experimental.pallas import tpu as pltpu
from jax.sharding import PartitionSpec as P

BLK = 128
PANEL = 512
WC = 2048
PC = 1024
CBB = 8
NB = PANEL // BLK
SUB = 8
F32 = jnp.float32
BF16 = jnp.bfloat16


def split(a):
    hi = a.astype(BF16)
    return hi, (a - hi.astype(F32)).astype(BF16)


def dot_nn(a, b):
    return lax.dot_general(a, b, (((1,), (0,)), ((), ())), preferred_element_type=F32)


def dot_nt(a, b):
    return lax.dot_general(a, b, (((1,), (1,)), ((), ())), preferred_element_type=F32)


def mm(dot, a, b):
    (ah, al), (bh, bl) = a, b
    return dot(ah, bh) + (dot(al, bh) + dot(ah, bl))


def lanes(v, j):
    return jnp.broadcast_to(v[:, j : j + 1], (SUB, BLK))


def sublanes(v, k):
    return jnp.broadcast_to(v[k : k + 1, :], (SUB, BLK))


def total(terms):
    while len(terms) > 1:
        terms = [a + b for a, b in zip(terms[::2], terms[1::2])] + terms[len(terms) // 2 * 2 :]
    return terms[0]


def factor_block(block, one):
    count = BLK // SUB
    span = count // 2
    width = span * SUB
    sub = lax.broadcasted_iota(jnp.int32, (SUB, BLK), 0)
    lane = lax.broadcasted_iota(jnp.int32, (SUB, BLK), 1)
    rows = [block[SUB * i : SUB * (i + 1), :] for i in range(count)]
    out = [None] * count
    for half in range(2):
        base = half * span
        now = rows[base : base + span]
        cols = None
        for g in range(span):
            first = SUB * (base + g)
            inside = (lane >= first) & (lane < first + SUB)
            follows = g + 1 < span
            if cols is None:
                cols = [lanes(now[g], first + k) * one for k in range(SUB)]
            if follows:
                kept = [lanes(now[g + 1], first + k) for k in range(SUB)]
                after = [lanes(now[g + 1], first + SUB + k) for k in range(SUB)]
                weights = [w * one for w in kept]
            head = jnp.where(inside, jnp.where(lane == first + sub, 1.0, 0.0), now[g])
            done = jnp.zeros((SUB, BLK), F32)
            for k in range(SUB):
                across = [sublanes(cols[q], k) if q >= k else None for q in range(SUB)]
                inv = 1.0 / across[k]
                here = sub == k
                row = sublanes(head, k)
                for q in range(k + 1, SUB):
                    step = jnp.where(here, -across[q], cols[k] * across[q])
                    cols[q] = jnp.where(here, 0.0, cols[q]) - step * inv
                step = jnp.where(here, -row, cols[k] * row)
                done = jnp.where(here, row * lax.rsqrt(across[k]), done)
                head = jnp.where(here, 0.0, head) - step * inv
                if follows:
                    scaled = weights[k] * inv
                    for q in range(k + 1, SUB):
                        weights[q] = weights[q] - scaled * across[q]
                    for q in range(SUB):
                        after[q] = after[q] - scaled * sublanes(weights[k], q)
            out[base + g] = done
            if base + g == count - 1:
                break
            spread = [sublanes(head, k) for k in range(SUB)]
            others = list(range(g + 1, span)) + (list(range(g)) if half == 0 else [])
            for i in others:
                mult = kept if i == g + 1 else [lanes(now[i], first + k) for k in range(SUB)]
                now[i] = jnp.where(inside, 0.0, now[i]) - total([m * r for m, r in zip(mult, spread)])
            now[g] = head
            cols = after if follows else None
        if half == 0:
            below = jnp.concatenate(rows[span:], axis=0)
            solved = jnp.concatenate(now + [jnp.zeros((BLK - width, BLK), F32)], axis=0)
            left = lax.broadcasted_iota(jnp.int32, below.shape, 1) < width
            below = jnp.where(left, 0.0, below) - mm(dot_nn, split(below), split(solved))
            rows[span:] = [below[SUB * i : SUB * (i + 1), :] for i in range(count - span)]
    return jnp.concatenate(out, axis=0)


def invert_panel(at, work, beside=None, saved=None):
    row = lax.broadcasted_iota(jnp.int32, (BLK, BLK), 0)
    col = lax.broadcasted_iota(jnp.int32, (BLK, BLK), 1)
    lane_block = lax.broadcasted_iota(jnp.int32, (BLK, PANEL), 1) // BLK
    one = jnp.full((SUB, BLK), 1.0, F32) * jnp.minimum(at[2], 1).astype(F32)

    def step(b, carry):
        here = pl.ds(pl.multiple_of(b * BLK, BLK), BLK)
        if beside is not None:
            beside(b)
        inv = jnp.where(row >= col, factor_block(work[b, :, here], one), 0.0)
        inv = split(inv) + (inv,)
        across = mm(dot_nn, inv[:2], split(work[b]))
        across = jnp.where(lane_block == b, jnp.concatenate([inv[2]] * NB, axis=1), across)
        across_parts = split(across)
        work[b] = across
        if saved is not None:
            for p in range(2):
                saved[0][p] = inv[p]
                saved[1][p] = across_parts[p]
        for i in range(1, NB):

            @pl.when(i > b)
            def _():
                below = split(mm(dot_nt, split(work[i, :, here]), inv[:2]))
                kept = jnp.where(lane_block == b, 0.0, work[i])
                work[i] = kept - mm(dot_nn, below, across_parts)

        return carry

    lax.fori_loop(0, NB, step, 0)


def lower_parts(work, parts, flipped=None):
    lane_block = lax.broadcasted_iota(jnp.int32, (BLK, PANEL), 1) // BLK
    for i in range(NB):
        rows = slice(i * BLK, (i + 1) * BLK)
        lower = jnp.where(lane_block <= i, work[i], 0.0)
        parts[0, rows, :], parts[1, rows, :] = split(lower)
        if flipped is not None:
            for j in range(NB):
                flip = split(lower[:, j * BLK : (j + 1) * BLK].T)
                for p in range(2):
                    flipped[p, j * BLK : (j + 1) * BLK, rows] = flip[p]


def take_pivot(at, blocks, work, sem):
    core = at[1] % 2

    for chip, own in enumerate(((0, 1), (1, 0), (3, 2), (2, 3))):

        @pl.when(at[1] // 2 == chip)
        def _():
            for i in range(2):
                for k in range(2):
                    pltpu.make_async_copy(blocks[4 * k + own[i]], work.at[2 * i + (core + k) % 2], sem).start()

    pltpu.make_async_copy(work, work, sem).wait()


def first_kernel(at, b0, b1, b2, b3, b4, b5, b6, b7, inv_out, work, inv, sem):
    take_pivot(at, (b0, b1, b2, b3, b4, b5, b6, b7), work, sem)
    invert_panel(at, work)
    lower_parts(work, inv.at[0], inv.at[1])
    copy = pltpu.make_async_copy(inv, inv_out, sem)
    copy.start()
    copy.wait()


def pair(ref, rows=slice(None)):
    return ref[0, rows, :], ref[1, rows, :]


def child_kernel(at, mid, own, inv0, factor, contribution, work, inv1, above, low_first, low_second, rows_second, own_first):
    upper = mid[NB:, :, :PANEL].reshape(PANEL, PANEL)
    upper_parts = split(upper)
    solved = split(mm(dot_nt, upper_parts, pair(inv0.at[0])))
    flipped = split(mm(dot_nt, pair(inv0.at[0]), upper_parts))
    above[0], above[1] = flipped
    second = mid[NB:, :, PANEL:].reshape(PANEL, PANEL) - mm(dot_nn, solved, flipped)
    work[...] = second.reshape(NB, BLK, PANEL)
    chunk = 2 * BLK // NB

    def beside(b):
        to = pl.ds(pl.multiple_of(b * BLK, BLK), BLK)
        part = split(mm(dot_nn, split(mid[b, :, :PANEL]), pair(inv0.at[1])))
        low_first[0, to, :], low_first[1, to, :] = part
        rows_second[to, :] = mid[b, :, PANEL:] - mm(dot_nn, part, pair(above))
        s = b // 2
        rows = pl.ds(pl.multiple_of((b % 2) * chunk, chunk), chunk)
        first = mm(dot_nn, split(own[s, rows, :PANEL]), pair(inv0.at[1]))
        factor[s, rows, :PANEL] = first
        part = split(first)
        to = pl.ds(pl.multiple_of(b * chunk, chunk), chunk)
        own_first[0, to, :], own_first[1, to, :] = part
        to = pl.ds(pl.multiple_of(PANEL + b * chunk, chunk), chunk)
        rows_second[to, :] = own[s, rows, PANEL:PC] - mm(dot_nn, part, pair(above))

    invert_panel(at, work, beside)
    lower_parts(work, inv1)
    result = mm(dot_nt, split(rows_second[...]), pair(inv1))
    low_second[0], low_second[1] = split(result[:PANEL])
    second = result[PANEL + BLK :]
    rest = own[1, :, PC : PC + PANEL] - mm(dot_nt, pair(own_first, slice(BLK, None)), pair(low_first))
    contribution[...] = (rest - mm(dot_nt, split(second), pair(low_second))).astype(BF16)
    factor[0, :, PANEL:] = jnp.where(at[1] < NB, 0.0, result[PANEL : PANEL + BLK])
    factor[1, :, PANEL:] = second


def place_row(row, r):
    own, back1, on1, back2, on2, back3, on3, back4, on4 = row
    whole = slice(0, BLK)
    low, high = slice(0, BLK // 2), slice(BLK // 2, BLK)
    return (
        [(own, whole)],
        [(on1, whole)],
        [(on2, whole)],
        [(on3, whole)],
        [(back4, low), (on4, high)],
        [(back3, whole)],
        [(back2, whole)],
        [(back1, whole)],
    )[r]


def pack_kernel(at, parent_of, owner_slot, *rest):
    row, outs, sem = rest[:9], rest[9:-1], rest[-1]
    y = at[0] // ZS
    z = at[0] % ZS
    total = jnp.int32(0)
    counts = [jnp.int32(0)] * (YS - 1)
    for r in range(ZS):
        slot = owner_slot[parent_of[y * ZS + (z + r) % ZS]]
        for s in range(1, YS):
            hit = slot == ((y + s) % YS) * ZS + z
            k = counts[s - 1]

            @pl.when(hit)
            def _():
                for source, rows in place_row(row, r):
                    pltpu.make_async_copy(source, outs[s - 1].at[k, rows], sem).start()

            counts[s - 1] = k + hit.astype(jnp.int32)
            total = total + hit.astype(jnp.int32)

    def wait(i, carry):
        pltpu.make_async_copy(row[0], outs[0].at[0], sem).wait()
        return carry

    lax.fori_loop(0, total, wait, 0)


def add_block(at, block_lists, c, block, out):
    t = block_lists[c, at[1]] // at[2]
    for k in range(NB):

        @pl.when(block_lists[c, k] == k)
        def _():
            cols = slice(k * BLK, (k + 1) * BLK)
            out[t, :, cols] = out[t, :, cols] + block[:, cols].astype(F32)


def add_all(at, block_lists, who, count, some_block, buf, out, sem):
    def wait(i, carry):
        pltpu.make_async_copy(some_block, buf.at[0], sem).wait()
        return carry

    def add(i, carry):
        add_block(at, block_lists, who[i], buf.at[i], out)
        return carry

    lax.fori_loop(0, count, wait, 0)
    lax.fori_loop(0, count, add, 0)


def near_kernel(at, parent_of, owner_slot, front_blocks, block_lists, entries, *rest):
    row, (out, buf, who, sem) = rest[:9], rest[9:]
    leaf = at[0]
    count = jnp.int32(0)
    for r in range(ZS):
        c = leaf // ZS * ZS + (leaf % ZS + r) % ZS
        hit = owner_slot[parent_of[c]] == leaf

        @pl.when(hit)
        def _():
            who[count] = c
            for source, rows in place_row(row, r):
                pltpu.make_async_copy(source, buf.at[count, rows], sem).start()

        count = count + hit.astype(jnp.int32)

    def find(q, live):
        return jnp.where(owner_slot[q] == leaf, front_blocks[q], live)

    live = lax.fori_loop(0, owner_slot.shape[0], find, jnp.int32(0))
    for t in range(entries.shape[0]):
        alive = t * at[2] + at[1] < live
        out[t] = jnp.where(alive, entries[t], 0.0)
    add_all(at, block_lists, who, count, row[0], buf, out, sem)


def far_kernel(at, parent_of, owner_slot, block_lists, started, *rest):
    others, (out, pivot, buf, who, sem) = rest[: YS - 1], rest[YS - 1 :]
    leaf = at[0]
    count = jnp.int32(0)
    for s in range(1, YS):
        y = (leaf // ZS + YS - s) % YS
        k = jnp.int32(0)
        for r in range(ZS):
            c = y * ZS + (leaf % ZS + r) % ZS
            hit = owner_slot[parent_of[c]] == leaf

            @pl.when(hit)
            def _():
                who[count] = c
                pltpu.make_async_copy(others[s - 1].at[k], buf.at[count], sem).start()

            k = k + hit.astype(jnp.int32)
            count = count + hit.astype(jnp.int32)

    for t in range(started.shape[0]):
        out[t] = started[t]
    add_all(at, block_lists, who, count, others[0].at[0], buf, out, sem)
    pivot[...] = out[0]


def parent_kernel(at, b0, b1, b2, b3, b4, b5, b6, b7, rows, factor, work, left, inv, across, sem):
    take_pivot(at, (b0, b1, b2, b3, b4, b5, b6, b7), work, sem)
    slots = rows.shape[0]
    left[...] = rows[...].reshape(slots * BLK, PANEL)
    inv[...] = jnp.zeros(inv.shape, BF16)
    across[...] = jnp.zeros(across.shape, BF16)

    def solve(b):
        here = pl.ds(pl.multiple_of(b * BLK, BLK), BLK)
        solved = mm(dot_nt, split(left[:, here]), pair(inv))
        factor[:, :, here] = solved.reshape(slots, BLK, BLK)
        return solved

    def beside(b):
        solved = solve(jnp.maximum(b - 1, 0))
        left[...] = left[...] - mm(dot_nn, split(solved), pair(across))

    invert_panel(at, work, beside, (inv, across))
    solve(NB - 1)


VMEM = pl.BlockSpec(memory_space=pltpu.VMEM)
SMEM = pl.BlockSpec(memory_space=pltpu.SMEM)
ANY = pl.BlockSpec(memory_space=pl.ANY)
HBM = pl.BlockSpec(memory_space=pltpu.HBM)
YS = 4
ZS = 8


def limit(mib):
    return pltpu.CompilerParams(vmem_limit_bytes=mib * 1024 * 1024)


def shape(*dims, dtype=F32):
    return jax.ShapeDtypeStruct(dims, dtype)


def chip_permute(x, pairs):
    return lax.ppermute(x, "panel", [(2 * a + c, 2 * b + c) for a, b in pairs for c in range(2)])


def gather_pivot(block):
    near = chip_permute(block, ((0, 1), (1, 0)))
    next_ = chip_permute(block, ((0, 3), (1, 2)))
    far = chip_permute(block, ((0, 2), (1, 3)))
    blocks = (block, near, next_, far)
    return blocks + tuple(lax.ppermute(b, "panel", [(i, i ^ 1) for i in range(8)]) for b in blocks)


def z_permute(x, s):
    return lax.ppermute(x, "leaf", [(y * ZS + z, y * ZS + (z + s) % ZS) for y in range(YS) for z in range(ZS)])


def along_z(own):
    back1, on1 = z_permute(own, 1), z_permute(own, -1)
    back2, on2 = z_permute(own, 2), z_permute(own, -2)
    back3, on3 = z_permute(back1, 2), z_permute(on1, -2)
    back4, on4 = z_permute(back2[: BLK // 2], 2), z_permute(on2[BLK // 2 :], -2)
    return own, back1, on1, back2, on2, back3, on3, back4, on4


def add_children(depth, at, tables, entries, row):
    parent_of, owner_slot, front_blocks, block_lists = tables
    sends = pl.pallas_call(
        pack_kernel,
        out_shape=(shape(depth, BLK, PANEL, dtype=BF16),) * (YS - 1),
        in_specs=[SMEM, SMEM, SMEM] + [ANY] * 9,
        out_specs=(ANY,) * (YS - 1),
        scratch_shapes=[pltpu.SemaphoreType.DMA],
        name=f"pack{depth}",
    )(at, parent_of, owner_slot, *row)
    others = []
    for s in range(1, YS):
        pairs = [(y * ZS + z, ((y + s) % YS) * ZS + z) for y in range(YS) for z in range(ZS)]
        others.append(lax.ppermute(sends[s - 1], "leaf", pairs))
    started = pl.pallas_call(
        near_kernel,
        out_shape=shape(*entries.shape),
        in_specs=[SMEM, SMEM, SMEM, SMEM, SMEM, VMEM] + [ANY] * 9,
        out_specs=VMEM,
        scratch_shapes=[pltpu.VMEM((ZS, BLK, PANEL), BF16), pltpu.SMEM((ZS,), jnp.int32), pltpu.SemaphoreType.DMA],
        compiler_params=limit(8),
        name=f"near{depth}",
    )(at, parent_of, owner_slot, front_blocks, block_lists, entries, *row)
    far = YS * ZS - ZS
    return pl.pallas_call(
        far_kernel,
        out_shape=(shape(*entries.shape), shape(BLK, PANEL)),
        in_specs=[SMEM, SMEM, SMEM, SMEM, VMEM] + [ANY] * (YS - 1),
        out_specs=(VMEM, VMEM),
        scratch_shapes=[pltpu.VMEM((far, BLK, PANEL), BF16), pltpu.SMEM((far,), jnp.int32), pltpu.SemaphoreType.DMA],
        compiler_params=limit(12),
        name=f"far{depth}",
    )(at, parent_of, owner_slot, block_lists, started, *others)


def on_device(child_front, parent_entries, parent_of, owner_slot, front_blocks, block_lists):
    panel_count = lax.axis_size("panel")
    panel = lax.axis_index("panel")
    leaf = lax.axis_index("leaf")
    parent_slots = parent_entries.shape[1]
    own = child_front.reshape(2, BLK, WC)
    with jax.named_scope("mid"):
        slot = (panel < NB).astype(jnp.int32)
        one = lax.dynamic_slice(own, (slot, jnp.int32(0), jnp.int32(0)), (1, BLK, PC))
        mid = lax.all_gather(one, "panel", axis=0, tiled=True)
    with jax.named_scope("pivot0"):
        blocks = gather_pivot(own[0, :, :PANEL])
    at = jnp.stack([leaf, panel, panel_count]).astype(jnp.int32)
    work = pltpu.VMEM((NB, BLK, PANEL), F32)
    parts = pltpu.VMEM((2, PANEL, PANEL), BF16)
    inv0 = pl.pallas_call(
        first_kernel,
        out_shape=shape(2, 2, PANEL, PANEL, dtype=BF16),
        in_specs=[SMEM] + [ANY] * 8,
        out_specs=HBM,
        scratch_shapes=[work, pltpu.VMEM((2, 2, PANEL, PANEL), BF16), pltpu.SemaphoreType.DMA],
        compiler_params=limit(12),
        name="first_panel",
    )(at, *[pltpu.with_memory_space_constraint(b, pltpu.HBM) for b in blocks])
    factor, contribution = pl.pallas_call(
        child_kernel,
        out_shape=(shape(2, BLK, PC), shape(BLK, PANEL, dtype=BF16)),
        in_specs=[SMEM, VMEM, VMEM, VMEM],
        out_specs=(VMEM, VMEM),
        scratch_shapes=[
            work,
            parts,
            parts,
            parts,
            parts,
            pltpu.VMEM((PANEL + 2 * BLK, PANEL), F32),
            pltpu.VMEM((2, 2 * BLK, PANEL), BF16),
        ],
        compiler_params=limit(28),
        name="child",
    )(at, mid, own, inv0)
    slots = jnp.sum(jnp.where(parent_of[:, None] == jnp.arange(owner_slot.shape[0])[None, :], owner_slot[None, :], 0), axis=1)
    hits = (slots[:, None] == jnp.arange(YS * ZS)[None, :]).reshape(YS, ZS, YS, ZS)
    counts = jnp.sum(hits.astype(jnp.int32), axis=1)
    elsewhere = jnp.arange(YS)[:, None, None] != jnp.arange(YS)[None, :, None]
    most = jnp.max(jnp.where(elsewhere, counts, 0))
    with jax.named_scope("along_z"):
        row = along_z(contribution)
    tables = (parent_of, owner_slot, front_blocks, block_lists)
    depths = (2, 3, ZS)
    with jax.named_scope("along_y"):
        assembled, pivot = lax.switch(
            (most > 2).astype(jnp.int32) + (most > 3).astype(jnp.int32),
            [lambda e, r, d=d: add_children(d, at, tables, e, r) for d in depths],
            parent_entries.reshape(parent_slots, BLK, PANEL),
            row,
        )
    with jax.named_scope("pivot2"):
        blocks = gather_pivot(pivot)
    parent_factor = pl.pallas_call(
        parent_kernel,
        out_shape=shape(parent_slots, BLK, PANEL),
        in_specs=[SMEM] + [ANY] * 8 + [VMEM],
        out_specs=VMEM,
        scratch_shapes=[
            work,
            pltpu.VMEM((parent_slots * BLK, PANEL), F32),
            pltpu.VMEM((2, BLK, BLK), BF16),
            pltpu.VMEM((2, BLK, PANEL), BF16),
            pltpu.SemaphoreType.DMA,
        ],
        compiler_params=limit(14),
        name="parent",
    )(at, *blocks, assembled)
    return (factor.reshape(child_front.shape[:-1] + (PC,)), parent_factor.reshape(parent_entries.shape))


def solution(mesh):
    front = P("leaf", None, "panel", None, None)
    return jax.shard_map(
        on_device,
        mesh=mesh,
        in_specs=(front, front, P(), P(), P(), P()),
        out_specs=(front, front),
        check_vma=False,
    )
```

```python
import functools

import jax
import jax.numpy as jnp
from jax import lax
from jax.experimental import pallas as pl
from jax.experimental.pallas import tpu as pltpu
from jax.sharding import PartitionSpec as P

BLK = 128
PANEL = 512
WC = 2048
PC = 1024
CBB = 8
NB = PANEL // BLK
SUB = 8
TILE = 16
TILES = BLK // TILE * NB
F32 = jnp.float32
BF16 = jnp.bfloat16


def split(a):
    hi = a.astype(BF16)
    return hi, (a - hi.astype(F32)).astype(BF16)


def dot_nn(a, b):
    return lax.dot_general(a, b, (((1,), (0,)), ((), ())), preferred_element_type=F32)


def dot_nt(a, b):
    return lax.dot_general(a, b, (((1,), (1,)), ((), ())), preferred_element_type=F32)


def mm(dot, a, b):
    (ah, al), (bh, bl) = a, b
    return dot(ah, bh) + (dot(al, bh) + dot(ah, bl))


def lanes(v, j):
    return jnp.broadcast_to(v[:, j : j + 1], (SUB, BLK))


def sublanes(v, k):
    return jnp.broadcast_to(v[k : k + 1, :], (SUB, BLK))


def total(terms):
    while len(terms) > 1:
        terms = [a + b for a, b in zip(terms[::2], terms[1::2])] + terms[len(terms) // 2 * 2 :]
    return terms[0]


def factor_block(block, one):
    count = BLK // SUB
    span = count // 2
    width = span * SUB
    sub = lax.broadcasted_iota(jnp.int32, (SUB, BLK), 0)
    lane = lax.broadcasted_iota(jnp.int32, (SUB, BLK), 1)
    rows = [block[SUB * i : SUB * (i + 1), :] for i in range(count)]
    out = [None] * count
    for half in range(2):
        base = half * span
        now = rows[base : base + span]
        cols = None
        for g in range(span):
            first = SUB * (base + g)
            inside = (lane >= first) & (lane < first + SUB)
            follows = g + 1 < span
            if cols is None:
                cols = [lanes(now[g], first + k) * one for k in range(SUB)]
            if follows:
                kept = [lanes(now[g + 1], first + k) for k in range(SUB)]
                after = [lanes(now[g + 1], first + SUB + k) for k in range(SUB)]
                weights = [w * one for w in kept]
            head = jnp.where(inside, jnp.where(lane == first + sub, 1.0, 0.0), now[g])
            done = jnp.zeros((SUB, BLK), F32)
            for k in range(SUB):
                across = [sublanes(cols[q], k) if q >= k else None for q in range(SUB)]
                inv = 1.0 / across[k]
                here = sub == k
                row = sublanes(head, k)
                for q in range(k + 1, SUB):
                    step = jnp.where(here, -across[q], cols[k] * across[q])
                    cols[q] = jnp.where(here, 0.0, cols[q]) - step * inv
                step = jnp.where(here, -row, cols[k] * row)
                done = jnp.where(here, row * lax.rsqrt(across[k]), done)
                head = jnp.where(here, 0.0, head) - step * inv
                if follows:
                    scaled = weights[k] * inv
                    for q in range(k + 1, SUB):
                        weights[q] = weights[q] - scaled * across[q]
                    for q in range(SUB):
                        after[q] = after[q] - scaled * sublanes(weights[k], q)
            out[base + g] = done
            if base + g == count - 1:
                break
            spread = [sublanes(head, k) for k in range(SUB)]
            others = list(range(g + 1, span)) + (list(range(g)) if half == 0 else [])
            for i in others:
                mult = kept if i == g + 1 else [lanes(now[i], first + k) for k in range(SUB)]
                now[i] = jnp.where(inside, 0.0, now[i]) - total([m * r for m, r in zip(mult, spread)])
            now[g] = head
            cols = after if follows else None
        if half == 0:
            below = jnp.concatenate(rows[span:], axis=0)
            solved = jnp.concatenate(now + [jnp.zeros((BLK - width, BLK), F32)], axis=0)
            left = lax.broadcasted_iota(jnp.int32, below.shape, 1) < width
            below = jnp.where(left, 0.0, below) - mm(dot_nn, split(below), split(solved))
            rows[span:] = [below[SUB * i : SUB * (i + 1), :] for i in range(count - span)]
    return jnp.concatenate(out, axis=0)


def invert_panel(at, work, beside=None):
    row = lax.broadcasted_iota(jnp.int32, (BLK, BLK), 0)
    col = lax.broadcasted_iota(jnp.int32, (BLK, BLK), 1)
    lane_block = lax.broadcasted_iota(jnp.int32, (BLK, PANEL), 1) // BLK
    one = jnp.full((SUB, BLK), 1.0, F32) * jnp.minimum(at[2], 1).astype(F32)

    def step(b, carry):
        here = pl.ds(pl.multiple_of(b * BLK, BLK), BLK)
        if beside is not None:
            beside(b)
        inv = jnp.where(row >= col, factor_block(work[b, :, here], one), 0.0)
        inv = split(inv) + (inv,)
        across = mm(dot_nn, inv[:2], split(work[b]))
        across = jnp.where(lane_block == b, jnp.concatenate([inv[2]] * NB, axis=1), across)
        across_parts = split(across)
        work[b] = across
        for i in range(1, NB):

            @pl.when(i > b)
            def _():
                below = split(mm(dot_nt, split(work[i, :, here]), inv[:2]))
                kept = jnp.where(lane_block == b, 0.0, work[i])
                work[i] = kept - mm(dot_nn, below, across_parts)

        return carry

    lax.fori_loop(0, NB, step, 0)


def lower_parts(work, parts, flipped=None):
    lane_block = lax.broadcasted_iota(jnp.int32, (BLK, PANEL), 1) // BLK
    for i in range(NB):
        rows = slice(i * BLK, (i + 1) * BLK)
        lower = jnp.where(lane_block <= i, work[i], 0.0)
        parts[0, rows, :], parts[1, rows, :] = split(lower)
        if flipped is not None:
            for j in range(NB):
                flip = split(lower[:, j * BLK : (j + 1) * BLK].T)
                for p in range(2):
                    flipped[p, j * BLK : (j + 1) * BLK, rows] = flip[p]


def take_pivot(at, blocks, work, sem=None):
    core = at[1] % 2

    for chip, own in enumerate(((0, 1), (1, 0), (3, 2), (2, 3))):

        @pl.when(at[1] // 2 == chip)
        def _():
            for i in range(2):
                for k in range(2):
                    source, to = blocks[4 * k + own[i]], work.at[2 * i + (core + k) % 2]
                    if sem is None:
                        to[...] = source[...]
                    else:
                        pltpu.make_async_copy(source, to, sem).start()

    if sem is not None:
        pltpu.make_async_copy(work, work, sem).wait()


def first_kernel(at, b0, b1, b2, b3, b4, b5, b6, b7, inv_out, work, inv, sem):
    take_pivot(at, (b0, b1, b2, b3, b4, b5, b6, b7), work, sem)
    invert_panel(at, work)
    lower_parts(work, inv.at[0], inv.at[1])
    copy = pltpu.make_async_copy(inv, inv_out, sem)
    copy.start()
    copy.wait()


def pair(ref, rows=slice(None)):
    return ref[0, rows, :], ref[1, rows, :]


def child_kernel(at, mid, own, inv0, factor, contribution, work, inv1, above, low_first, low_second, rows_second, own_first):
    upper = mid[NB:, :, :PANEL].reshape(PANEL, PANEL)
    upper_parts = split(upper)
    solved = split(mm(dot_nt, upper_parts, pair(inv0.at[0])))
    flipped = split(mm(dot_nt, pair(inv0.at[0]), upper_parts))
    above[0], above[1] = flipped
    second = mid[NB:, :, PANEL:].reshape(PANEL, PANEL) - mm(dot_nn, solved, flipped)
    work[...] = second.reshape(NB, BLK, PANEL)
    chunk = 2 * BLK // NB

    def beside(b):
        to = pl.ds(pl.multiple_of(b * BLK, BLK), BLK)
        part = split(mm(dot_nn, split(mid[b, :, :PANEL]), pair(inv0.at[1])))
        low_first[0, to, :], low_first[1, to, :] = part
        rows_second[to, :] = mid[b, :, PANEL:] - mm(dot_nn, part, pair(above))
        s = b // 2
        rows = pl.ds(pl.multiple_of((b % 2) * chunk, chunk), chunk)
        first = mm(dot_nn, split(own[s, rows, :PANEL]), pair(inv0.at[1]))
        factor[s, rows, :PANEL] = first
        part = split(first)
        to = pl.ds(pl.multiple_of(b * chunk, chunk), chunk)
        own_first[0, to, :], own_first[1, to, :] = part
        to = pl.ds(pl.multiple_of(PANEL + b * chunk, chunk), chunk)
        rows_second[to, :] = own[s, rows, PANEL:PC] - mm(dot_nn, part, pair(above))

    invert_panel(at, work, beside)
    lower_parts(work, inv1)
    result = mm(dot_nt, split(rows_second[...]), pair(inv1))
    low_second[0], low_second[1] = split(result[:PANEL])
    second = result[PANEL + BLK :]
    rest = own[1, :, PC : PC + PANEL] - mm(dot_nt, pair(own_first, slice(BLK, None)), pair(low_first))
    rest = (rest - mm(dot_nt, split(second), pair(low_second))).astype(BF16)
    for i in range(TILES):
        r, k = i // NB * TILE, i % NB * BLK
        contribution[i] = rest[r : r + TILE, k : k + BLK]
    factor[0, :, PANEL:] = jnp.where(at[1] < NB, 0.0, result[PANEL : PANEL + BLK])
    factor[1, :, PANEL:] = second


def pack_kernel(at, parent_of, owner_slot, tiles, out, count):
    def clear(s, carry):
        count[s] = 0
        return carry

    def place(c, carry):
        slot = owner_slot[parent_of[c]]
        out[slot, count[slot]] = tiles[c]
        count[slot] = count[slot] + 1
        return carry

    lax.fori_loop(0, out.shape[0], clear, 0)
    lax.fori_loop(0, tiles.shape[0], place, 0)


def assemble_kernel(at, parent_of, owner_slot, front_blocks, block_lists, entries, tiles, out, pivot):
    leaf = at[0]

    def find(q, live):
        return jnp.where(owner_slot[q] == leaf, front_blocks[q], live)

    live = lax.fori_loop(0, owner_slot.shape[0], find, jnp.int32(0))
    for t in range(entries.shape[0]):
        alive = t * at[2] + at[1] < live
        out[t] = jnp.where(alive, entries[t], 0.0)

    def add(c, k):
        hit = owner_slot[parent_of[c]] == leaf

        @pl.when(hit)
        def _():
            t = block_lists[c, at[1]] // at[2]
            for b in range(NB):

                @pl.when(block_lists[c, b] == b)
                def _():
                    for i in range(b, TILES, NB):
                        rows, cols = slice(i // NB * TILE, (i // NB + 1) * TILE), slice(b * BLK, (b + 1) * BLK)
                        out[t, rows, cols] = out[t, rows, cols] + tiles[i, k].astype(F32)

        return k + hit.astype(jnp.int32)

    lax.fori_loop(0, parent_of.shape[0], add, jnp.int32(0))
    pivot[...] = out[0]


def parent_kernel(at, b0, b1, b2, b3, b4, b5, b6, b7, rows, factor, work, inv):
    take_pivot(at, (b0, b1, b2, b3, b4, b5, b6, b7), work)
    invert_panel(at, work)
    lower_parts(work, inv)
    slots = rows.shape[0]
    solved = mm(dot_nt, split(rows[...].reshape(slots * BLK, PANEL)), pair(inv))
    factor[...] = solved.reshape(slots, BLK, PANEL)


VMEM = pl.BlockSpec(memory_space=pltpu.VMEM)
SMEM = pl.BlockSpec(memory_space=pltpu.SMEM)
ANY = pl.BlockSpec(memory_space=pl.ANY)
HBM = pl.BlockSpec(memory_space=pltpu.HBM)


def limit(mib):
    return pltpu.CompilerParams(vmem_limit_bytes=mib * 1024 * 1024)


def shape(*dims, dtype=F32):
    return jax.ShapeDtypeStruct(dims, dtype)


def chip_permute(x, pairs):
    return lax.ppermute(x, "panel", [(2 * a + c, 2 * b + c) for a, b in pairs for c in range(2)])


def gather_pivot(block):
    near = chip_permute(block, ((0, 1), (1, 0)))
    next_ = chip_permute(block, ((0, 3), (1, 2)))
    far = chip_permute(block, ((0, 2), (1, 3)))
    blocks = (block, near, next_, far)
    return blocks + tuple(lax.ppermute(b, "panel", [(i, i ^ 1) for i in range(8)]) for b in blocks)


def add_children(depth, at, tables, entries, tiles):
    parent_of, owner_slot, front_blocks, block_lists = tables
    sends = pl.pallas_call(
        pack_kernel,
        out_shape=shape(TILES, depth, TILE, BLK, dtype=BF16),
        in_specs=[SMEM, SMEM, SMEM, VMEM],
        out_specs=VMEM,
        scratch_shapes=[pltpu.SMEM((TILES,), jnp.int32)],
        compiler_params=limit(8),
        name=f"pack{depth}",
    )(at, parent_of, owner_slot, tiles)
    mine = lax.all_to_all(sends, "leaf", 0, 0, tiled=True)
    return pl.pallas_call(
        assemble_kernel,
        out_shape=(shape(*entries.shape), shape(BLK, PANEL)),
        in_specs=[SMEM, SMEM, SMEM, SMEM, SMEM, VMEM, VMEM],
        out_specs=(VMEM, VMEM),
        compiler_params=limit(12),
        name=f"assemble{depth}",
    )(at, parent_of, owner_slot, front_blocks, block_lists, entries, mine)


def on_device(child_front, parent_entries, parent_of, owner_slot, front_blocks, block_lists):
    panel_count = lax.axis_size("panel")
    panel = lax.axis_index("panel")
    leaf = lax.axis_index("leaf")
    parent_slots = parent_entries.shape[1]
    own = child_front.reshape(2, BLK, WC)
    with jax.named_scope("mid"):
        slot = (panel < NB).astype(jnp.int32)
        one = lax.dynamic_slice(own, (slot, jnp.int32(0), jnp.int32(0)), (1, BLK, PC))
        mid = lax.all_gather(one, "panel", axis=0, tiled=True)
    with jax.named_scope("pivot0"):
        blocks = gather_pivot(own[0, :, :PANEL])
    at = jnp.stack([leaf, panel, panel_count]).astype(jnp.int32)
    work = pltpu.VMEM((NB, BLK, PANEL), F32)
    parts = pltpu.VMEM((2, PANEL, PANEL), BF16)
    inv0 = pl.pallas_call(
        first_kernel,
        out_shape=shape(2, 2, PANEL, PANEL, dtype=BF16),
        in_specs=[SMEM] + [ANY] * 8,
        out_specs=HBM,
        scratch_shapes=[work, pltpu.VMEM((2, 2, PANEL, PANEL), BF16), pltpu.SemaphoreType.DMA],
        compiler_params=limit(12),
        name="first_panel",
    )(at, *[pltpu.with_memory_space_constraint(b, pltpu.HBM) for b in blocks])
    factor, contribution = pl.pallas_call(
        child_kernel,
        out_shape=(shape(2, BLK, PC), shape(TILES, TILE, BLK, dtype=BF16)),
        in_specs=[SMEM, VMEM, VMEM, VMEM],
        out_specs=(VMEM, VMEM),
        scratch_shapes=[
            work,
            parts,
            parts,
            parts,
            parts,
            pltpu.VMEM((PANEL + 2 * BLK, PANEL), F32),
            pltpu.VMEM((2, 2 * BLK, PANEL), BF16),
        ],
        compiler_params=limit(28),
        name="child",
    )(at, mid, own, inv0)
    slots = jnp.sum(jnp.where(parent_of[:, None] == jnp.arange(owner_slot.shape[0])[None, :], owner_slot[None, :], 0), axis=1)
    most = jnp.max(jnp.sum((slots[:, None] == jnp.arange(TILES)[None, :]).astype(jnp.int32), axis=0))
    with jax.named_scope("tiles"):
        tiles = lax.all_to_all(contribution, "leaf", 0, 0, tiled=True)
    tables = (parent_of, owner_slot, front_blocks, block_lists)
    depths = (4, 6, parent_of.shape[0])
    with jax.named_scope("children"):
        assembled, pivot = lax.switch(
            (most > depths[0]).astype(jnp.int32) + (most > depths[1]).astype(jnp.int32),
            [lambda e, r, d=d: add_children(d, at, tables, e, r) for d in depths],
            parent_entries.reshape(parent_slots, BLK, PANEL),
            tiles,
        )
    with jax.named_scope("pivot2"):
        blocks = gather_pivot(pivot)
    parent_factor = pl.pallas_call(
        parent_kernel,
        out_shape=shape(parent_slots, BLK, PANEL),
        in_specs=[SMEM] + [VMEM] * 9,
        out_specs=VMEM,
        scratch_shapes=[
            work,
            parts,
        ],
        compiler_params=limit(14),
        name="parent",
    )(at, *blocks, assembled)
    return (factor.reshape(child_front.shape[:-1] + (PC,)), parent_factor.reshape(parent_entries.shape))


def solution(mesh):
    front = P("leaf", None, "panel", None, None)
    return jax.shard_map(
        on_device,
        mesh=mesh,
        in_specs=(front, front, P(), P(), P(), P()),
        out_specs=(front, front),
        check_vma=False,
    )
```

```python
import functools

import jax
import jax.numpy as jnp
from jax import lax
from jax.experimental import pallas as pl
from jax.experimental.pallas import tpu as pltpu
from jax.sharding import PartitionSpec as P

BLK = 128
PANEL = 512
WC = 2048
PC = 1024
CBB = 8
NB = PANEL // BLK
SUB = 8
TILE = 16
TILES = BLK // TILE * NB
F32 = jnp.float32
BF16 = jnp.bfloat16


def split(a):
    hi = a.astype(BF16)
    return hi, (a - hi.astype(F32)).astype(BF16)


def dot_nn(a, b):
    return lax.dot_general(a, b, (((1,), (0,)), ((), ())), preferred_element_type=F32)


def dot_nt(a, b):
    return lax.dot_general(a, b, (((1,), (1,)), ((), ())), preferred_element_type=F32)


def mm(dot, a, b):
    (ah, al), (bh, bl) = a, b
    return dot(ah, bh) + (dot(al, bh) + dot(ah, bl))


def lanes(v, j):
    return jnp.broadcast_to(v[:, j : j + 1], (SUB, BLK))


def sublanes(v, k):
    return jnp.broadcast_to(v[k : k + 1, :], (SUB, BLK))


def total(terms):
    while len(terms) > 1:
        terms = [a + b for a, b in zip(terms[::2], terms[1::2])] + terms[len(terms) // 2 * 2 :]
    return terms[0]


def factor_block(block, one):
    count = BLK // SUB
    span = count // 2
    width = span * SUB
    sub = lax.broadcasted_iota(jnp.int32, (SUB, BLK), 0)
    lane = lax.broadcasted_iota(jnp.int32, (SUB, BLK), 1)
    rows = [block[SUB * i : SUB * (i + 1), :] for i in range(count)]
    out = [None] * count
    for half in range(2):
        base = half * span
        now = rows[base : base + span]
        cols = None
        for g in range(span):
            first = SUB * (base + g)
            inside = (lane >= first) & (lane < first + SUB)
            follows = g + 1 < span
            if cols is None:
                cols = [lanes(now[g], first + k) * one for k in range(SUB)]
            if follows:
                kept = [lanes(now[g + 1], first + k) for k in range(SUB)]
                after = [lanes(now[g + 1], first + SUB + k) for k in range(SUB)]
                weights = [w * one for w in kept]
            head = jnp.where(inside, jnp.where(lane == first + sub, 1.0, 0.0), now[g])
            done = jnp.zeros((SUB, BLK), F32)
            for k in range(SUB):
                across = [sublanes(cols[q], k) if q >= k else None for q in range(SUB)]
                inv = 1.0 / across[k]
                here = sub == k
                row = sublanes(head, k)
                for q in range(k + 1, SUB):
                    step = jnp.where(here, -across[q], cols[k] * across[q])
                    cols[q] = jnp.where(here, 0.0, cols[q]) - step * inv
                step = jnp.where(here, -row, cols[k] * row)
                done = jnp.where(here, row * lax.rsqrt(across[k]), done)
                head = jnp.where(here, 0.0, head) - step * inv
                if follows:
                    scaled = weights[k] * inv
                    for q in range(k + 1, SUB):
                        weights[q] = weights[q] - scaled * across[q]
                    for q in range(SUB):
                        after[q] = after[q] - scaled * sublanes(weights[k], q)
            out[base + g] = done
            if base + g == count - 1:
                break
            spread = [sublanes(head, k) for k in range(SUB)]
            others = list(range(g + 1, span)) + (list(range(g)) if half == 0 else [])
            for i in others:
                mult = kept if i == g + 1 else [lanes(now[i], first + k) for k in range(SUB)]
                now[i] = jnp.where(inside, 0.0, now[i]) - total([m * r for m, r in zip(mult, spread)])
            now[g] = head
            cols = after if follows else None
        if half == 0:
            below = jnp.concatenate(rows[span:], axis=0)
            solved = jnp.concatenate(now + [jnp.zeros((BLK - width, BLK), F32)], axis=0)
            left = lax.broadcasted_iota(jnp.int32, below.shape, 1) < width
            below = jnp.where(left, 0.0, below) - mm(dot_nn, split(below), split(solved))
            rows[span:] = [below[SUB * i : SUB * (i + 1), :] for i in range(count - span)]
    return jnp.concatenate(out, axis=0)


def invert_panel(at, work, beside=None):
    row = lax.broadcasted_iota(jnp.int32, (BLK, BLK), 0)
    col = lax.broadcasted_iota(jnp.int32, (BLK, BLK), 1)
    lane_block = lax.broadcasted_iota(jnp.int32, (BLK, PANEL), 1) // BLK
    row_block = lax.broadcasted_iota(jnp.int32, (PANEL - BLK, 1), 0) // BLK + 1
    later_block = lax.broadcasted_iota(jnp.int32, (PANEL - BLK, PANEL), 1) // BLK
    one = jnp.full((SUB, BLK), 1.0, F32) * jnp.minimum(at[2], 1).astype(F32)

    def step(b, carry):
        here = pl.ds(pl.multiple_of(b * BLK, BLK), BLK)
        if beside is not None:
            beside(b)
        inv = jnp.where(row >= col, factor_block(work[b, :, here], one), 0.0)
        inv = split(inv) + (inv,)
        across = mm(dot_nn, inv[:2], split(work[b]))
        across = jnp.where(lane_block == b, jnp.concatenate([inv[2]] * NB, axis=1), across)
        across_parts = split(across)
        work[b] = across

        @pl.when(b < NB - 1)
        def _():
            later = work[1:].reshape(PANEL - BLK, PANEL)
            mine = work[1:, :, here].reshape(PANEL - BLK, BLK)
            below = jnp.where(row_block > b, mm(dot_nt, split(mine), inv[:2]), 0.0)
            kept = jnp.where((row_block > b) & (later_block == b), 0.0, later)
            work[1:] = (kept - mm(dot_nn, split(below), across_parts)).reshape(NB - 1, BLK, PANEL)

        return carry

    lax.fori_loop(0, NB, step, 0)


def lower_parts(work, parts, flipped=None):
    lane_block = lax.broadcasted_iota(jnp.int32, (BLK, PANEL), 1) // BLK
    for i in range(NB):
        rows = slice(i * BLK, (i + 1) * BLK)
        lower = jnp.where(lane_block <= i, work[i], 0.0)
        parts[0, rows, :], parts[1, rows, :] = split(lower)
        if flipped is not None:
            for j in range(NB):
                flip = split(lower[:, j * BLK : (j + 1) * BLK].T)
                for p in range(2):
                    flipped[p, j * BLK : (j + 1) * BLK, rows] = flip[p]


def take_pivot(at, blocks, work, sem=None):
    core = at[1] % 2

    for chip, own in enumerate(((0, 1), (1, 0), (3, 2), (2, 3))):

        @pl.when(at[1] // 2 == chip)
        def _():
            for i in range(2):
                for k in range(2):
                    source, to = blocks[4 * k + own[i]], work.at[2 * i + (core + k) % 2]
                    if sem is None:
                        to[...] = source[...]
                    else:
                        pltpu.make_async_copy(source, to, sem).start()

    if sem is not None:
        pltpu.make_async_copy(work, work, sem).wait()


def first_kernel(at, b0, b1, b2, b3, b4, b5, b6, b7, inv_out, work, inv, sem):
    take_pivot(at, (b0, b1, b2, b3, b4, b5, b6, b7), work, sem)
    invert_panel(at, work)
    lower_parts(work, inv.at[0], inv.at[1])
    copy = pltpu.make_async_copy(inv, inv_out, sem)
    copy.start()
    copy.wait()


def pair(ref, rows=slice(None)):
    return ref[0, rows, :], ref[1, rows, :]


def child_kernel(at, mid, own_far, inv0, factor, contribution, own, work, inv1, above, low_first, low_second, rows_second, own_first, sem):
    fetch = pltpu.make_async_copy(own_far.at[:, :, : PC + PANEL], own, sem)
    fetch.start()
    upper = mid[NB:, :, :PANEL].reshape(PANEL, PANEL)
    upper_parts = split(upper)
    solved = split(mm(dot_nt, upper_parts, pair(inv0.at[0])))
    flipped = split(mm(dot_nt, pair(inv0.at[0]), upper_parts))
    above[0], above[1] = flipped
    second = mid[NB:, :, PANEL:].reshape(PANEL, PANEL) - mm(dot_nn, solved, flipped)
    work[...] = second.reshape(NB, BLK, PANEL)
    chunk = 2 * BLK // NB
    fetch.wait()

    def beside(b):
        to = pl.ds(pl.multiple_of(b * BLK, BLK), BLK)
        part = split(mm(dot_nn, split(mid[b, :, :PANEL]), pair(inv0.at[1])))
        low_first[0, to, :], low_first[1, to, :] = part
        rows_second[to, :] = mid[b, :, PANEL:] - mm(dot_nn, part, pair(above))
        s = b // 2
        rows = pl.ds(pl.multiple_of((b % 2) * chunk, chunk), chunk)
        first = mm(dot_nn, split(own[s, rows, :PANEL]), pair(inv0.at[1]))
        factor[s, rows, :PANEL] = first
        part = split(first)
        to = pl.ds(pl.multiple_of(b * chunk, chunk), chunk)
        own_first[0, to, :], own_first[1, to, :] = part
        to = pl.ds(pl.multiple_of(PANEL + b * chunk, chunk), chunk)
        rows_second[to, :] = own[s, rows, PANEL:PC] - mm(dot_nn, part, pair(above))

    invert_panel(at, work, beside)
    lower_parts(work, inv1)
    result = mm(dot_nt, split(rows_second[...]), pair(inv1))
    low_second[0], low_second[1] = split(result[:PANEL])
    second = result[PANEL + BLK :]
    rest = own[1, :, PC : PC + PANEL] - mm(dot_nt, pair(own_first, slice(BLK, None)), pair(low_first))
    rest = (rest - mm(dot_nt, split(second), pair(low_second))).astype(BF16)
    for i in range(TILES):
        r, k = i // NB * TILE, i % NB * BLK
        contribution[i] = rest[r : r + TILE, k : k + BLK]
    factor[0, :, PANEL:] = jnp.where(at[1] < NB, 0.0, result[PANEL : PANEL + BLK])
    factor[1, :, PANEL:] = second


def pack_kernel(at, parent_of, owner_slot, tiles, out, count):
    def clear(s, carry):
        count[s] = 0
        return carry

    def place(c, carry):
        slot = owner_slot[parent_of[c]]
        out[slot, count[slot]] = tiles[c]
        count[slot] = count[slot] + 1
        return carry

    lax.fori_loop(0, out.shape[0], clear, 0)
    lax.fori_loop(0, tiles.shape[0], place, 0)


def assemble_kernel(at, parent_of, owner_slot, front_blocks, block_lists, entries, tiles, out, pivot):
    leaf = at[0]

    def find(q, live):
        return jnp.where(owner_slot[q] == leaf, front_blocks[q], live)

    live = lax.fori_loop(0, owner_slot.shape[0], find, jnp.int32(0))
    for t in range(entries.shape[0]):
        alive = t * at[2] + at[1] < live
        out[t] = jnp.where(alive, entries[t], 0.0)

    def add(c, k):
        hit = owner_slot[parent_of[c]] == leaf

        @pl.when(hit)
        def _():
            t = block_lists[c, at[1]] // at[2]
            for b in range(NB):

                @pl.when(block_lists[c, b] == b)
                def _():
                    for i in range(b, TILES, NB):
                        rows, cols = slice(i // NB * TILE, (i // NB + 1) * TILE), slice(b * BLK, (b + 1) * BLK)
                        out[t, rows, cols] = out[t, rows, cols] + tiles[i, k].astype(F32)

        return k + hit.astype(jnp.int32)

    lax.fori_loop(0, parent_of.shape[0], add, jnp.int32(0))
    pivot[...] = out[0]


def parent_kernel(at, b0, b1, b2, b3, b4, b5, b6, b7, rows, factor, work, inv):
    take_pivot(at, (b0, b1, b2, b3, b4, b5, b6, b7), work)
    invert_panel(at, work)
    lower_parts(work, inv)
    slots = rows.shape[0]
    solved = mm(dot_nt, split(rows[...].reshape(slots * BLK, PANEL)), pair(inv))
    factor[...] = solved.reshape(slots, BLK, PANEL)


VMEM = pl.BlockSpec(memory_space=pltpu.VMEM)
SMEM = pl.BlockSpec(memory_space=pltpu.SMEM)
ANY = pl.BlockSpec(memory_space=pl.ANY)
HBM = pl.BlockSpec(memory_space=pltpu.HBM)


def limit(mib):
    return pltpu.CompilerParams(vmem_limit_bytes=mib * 1024 * 1024)


def shape(*dims, dtype=F32):
    return jax.ShapeDtypeStruct(dims, dtype)


def chip_permute(x, pairs):
    return lax.ppermute(x, "panel", [(2 * a + c, 2 * b + c) for a, b in pairs for c in range(2)])


def gather_pivot(block):
    near = chip_permute(block, ((0, 1), (1, 0)))
    next_ = chip_permute(block, ((0, 3), (1, 2)))
    far = chip_permute(block, ((0, 2), (1, 3)))
    blocks = (block, near, next_, far)
    return blocks + tuple(lax.ppermute(b, "panel", [(i, i ^ 1) for i in range(8)]) for b in blocks)


def add_children(depth, at, tables, entries, tiles):
    parent_of, owner_slot, front_blocks, block_lists = tables
    sends = pl.pallas_call(
        pack_kernel,
        out_shape=shape(TILES, depth, TILE, BLK, dtype=BF16),
        in_specs=[SMEM, SMEM, SMEM, VMEM],
        out_specs=VMEM,
        scratch_shapes=[pltpu.SMEM((TILES,), jnp.int32)],
        compiler_params=limit(8),
        name=f"pack{depth}",
    )(at, parent_of, owner_slot, tiles)
    mine = lax.all_to_all(sends, "leaf", 0, 0, tiled=True)
    return pl.pallas_call(
        assemble_kernel,
        out_shape=(shape(*entries.shape), shape(BLK, PANEL)),
        in_specs=[SMEM, SMEM, SMEM, SMEM, SMEM, VMEM, VMEM],
        out_specs=(VMEM, VMEM),
        compiler_params=limit(12),
        name=f"assemble{depth}",
    )(at, parent_of, owner_slot, front_blocks, block_lists, entries, mine)


def on_device(child_front, parent_entries, parent_of, owner_slot, front_blocks, block_lists):
    panel_count = lax.axis_size("panel")
    panel = lax.axis_index("panel")
    leaf = lax.axis_index("leaf")
    parent_slots = parent_entries.shape[1]
    own = child_front.reshape(2, BLK, WC)
    with jax.named_scope("mid"):
        slot = (panel < NB).astype(jnp.int32)
        one = lax.dynamic_slice(own, (slot, jnp.int32(0), jnp.int32(0)), (1, BLK, PC))
        mid = lax.all_gather(one, "panel", axis=0, tiled=True)
    with jax.named_scope("pivot0"):
        blocks = gather_pivot(own[0, :, :PANEL])
    at = jnp.stack([leaf, panel, panel_count]).astype(jnp.int32)
    work = pltpu.VMEM((NB, BLK, PANEL), F32)
    parts = pltpu.VMEM((2, PANEL, PANEL), BF16)
    inv0 = pl.pallas_call(
        first_kernel,
        out_shape=shape(2, 2, PANEL, PANEL, dtype=BF16),
        in_specs=[SMEM] + [ANY] * 8,
        out_specs=HBM,
        scratch_shapes=[work, pltpu.VMEM((2, 2, PANEL, PANEL), BF16), pltpu.SemaphoreType.DMA],
        compiler_params=limit(12),
        name="first_panel",
    )(at, *[pltpu.with_memory_space_constraint(b, pltpu.HBM) for b in blocks])
    factor, contribution = pl.pallas_call(
        child_kernel,
        out_shape=(shape(2, BLK, PC), shape(TILES, TILE, BLK, dtype=BF16)),
        in_specs=[SMEM, VMEM, HBM, VMEM],
        out_specs=(VMEM, VMEM),
        scratch_shapes=[
            pltpu.VMEM((2, BLK, PC + PANEL), F32),
            work,
            parts,
            parts,
            parts,
            parts,
            pltpu.VMEM((PANEL + 2 * BLK, PANEL), F32),
            pltpu.VMEM((2, 2 * BLK, PANEL), BF16),
            pltpu.SemaphoreType.DMA,
        ],
        compiler_params=limit(28),
        name="child",
    )(at, mid, pltpu.with_memory_space_constraint(own, pltpu.HBM), inv0)
    slots = jnp.sum(jnp.where(parent_of[:, None] == jnp.arange(owner_slot.shape[0])[None, :], owner_slot[None, :], 0), axis=1)
    most = jnp.max(jnp.sum((slots[:, None] == jnp.arange(TILES)[None, :]).astype(jnp.int32), axis=0))
    with jax.named_scope("tiles"):
        tiles = lax.all_to_all(contribution, "leaf", 0, 0, tiled=True)
    tables = (parent_of, owner_slot, front_blocks, block_lists)
    depths = (4, 6, parent_of.shape[0])
    with jax.named_scope("children"):
        assembled, pivot = lax.switch(
            (most > depths[0]).astype(jnp.int32) + (most > depths[1]).astype(jnp.int32),
            [lambda e, r, d=d: add_children(d, at, tables, e, r) for d in depths],
            parent_entries.reshape(parent_slots, BLK, PANEL),
            tiles,
        )
    with jax.named_scope("pivot2"):
        blocks = gather_pivot(pivot)
    parent_factor = pl.pallas_call(
        parent_kernel,
        out_shape=shape(parent_slots, BLK, PANEL),
        in_specs=[SMEM] + [VMEM] * 9,
        out_specs=VMEM,
        scratch_shapes=[
            work,
            parts,
        ],
        compiler_params=limit(14),
        name="parent",
    )(at, *blocks, assembled)
    return (factor.reshape(child_front.shape[:-1] + (PC,)), parent_factor.reshape(parent_entries.shape))


def solution(mesh):
    front = P("leaf", None, "panel", None, None)
    return jax.shard_map(
        on_device,
        mesh=mesh,
        in_specs=(front, front, P(), P(), P(), P()),
        out_specs=(front, front),
        check_vma=False,
    )
```

```python
import functools

import jax
import jax.numpy as jnp
from jax import lax
from jax.experimental import pallas as pl
from jax.experimental.pallas import tpu as pltpu
from jax.sharding import PartitionSpec as P

BLK = 128
PANEL = 512
WC = 2048
PC = 1024
CBB = 8
NB = PANEL // BLK
SUB = 8
TILE = 16
TILES = BLK // TILE * NB
F32 = jnp.float32
BF16 = jnp.bfloat16


def split(a):
    hi = a.astype(BF16)
    return hi, (a - hi.astype(F32)).astype(BF16)


def dot_nn(a, b):
    return lax.dot_general(a, b, (((1,), (0,)), ((), ())), preferred_element_type=F32)


def dot_nt(a, b):
    return lax.dot_general(a, b, (((1,), (1,)), ((), ())), preferred_element_type=F32)


def mm(dot, a, b):
    (ah, al), (bh, bl) = a, b
    return dot(ah, bh) + (dot(al, bh) + dot(ah, bl))


def lanes(v, j):
    return jnp.broadcast_to(v[:, j : j + 1], (SUB, BLK))


def sublanes(v, k):
    return jnp.broadcast_to(v[k : k + 1, :], (SUB, BLK))


def total(terms):
    while len(terms) > 1:
        terms = [a + b for a, b in zip(terms[::2], terms[1::2])] + terms[len(terms) // 2 * 2 :]
    return terms[0]


def factor_block(block, one):
    count = BLK // SUB
    span = count // 2
    width = span * SUB
    sub = lax.broadcasted_iota(jnp.int32, (SUB, BLK), 0)
    lane = lax.broadcasted_iota(jnp.int32, (SUB, BLK), 1)
    rows = [block[SUB * i : SUB * (i + 1), :] for i in range(count)]
    out = [None] * count
    for half in range(2):
        base = half * span
        now = rows[base : base + span]
        cols = None
        for g in range(span):
            first = SUB * (base + g)
            inside = (lane >= first) & (lane < first + SUB)
            follows = g + 1 < span
            if cols is None:
                cols = [lanes(now[g], first + k) * one for k in range(SUB)]
            if follows:
                kept = [lanes(now[g + 1], first + k) for k in range(SUB)]
                after = [lanes(now[g + 1], first + SUB + k) for k in range(SUB)]
                weights = [w * one for w in kept]
            head = jnp.where(inside, jnp.where(lane == first + sub, 1.0, 0.0), now[g])
            done = jnp.zeros((SUB, BLK), F32)
            for k in range(SUB):
                across = [sublanes(cols[q], k) if q >= k else None for q in range(SUB)]
                inv = 1.0 / across[k]
                here = sub == k
                row = sublanes(head, k)
                for q in range(k + 1, SUB):
                    step = jnp.where(here, -across[q], cols[k] * across[q])
                    cols[q] = jnp.where(here, 0.0, cols[q]) - step * inv
                step = jnp.where(here, -row, cols[k] * row)
                done = jnp.where(here, row * lax.rsqrt(across[k]), done)
                head = jnp.where(here, 0.0, head) - step * inv
                if follows:
                    scaled = weights[k] * inv
                    for q in range(k + 1, SUB):
                        weights[q] = weights[q] - scaled * across[q]
                    for q in range(SUB):
                        after[q] = after[q] - scaled * sublanes(weights[k], q)
            out[base + g] = done
            if base + g == count - 1:
                break
            spread = [sublanes(head, k) for k in range(SUB)]
            others = list(range(g + 1, span)) + (list(range(g)) if half == 0 else [])
            for i in others:
                mult = kept if i == g + 1 else [lanes(now[i], first + k) for k in range(SUB)]
                now[i] = jnp.where(inside, 0.0, now[i]) - total([m * r for m, r in zip(mult, spread)])
            now[g] = head
            cols = after if follows else None
        if half == 0:
            below = jnp.concatenate(rows[span:], axis=0)
            solved = jnp.concatenate(now + [jnp.zeros((BLK - width, BLK), F32)], axis=0)
            left = lax.broadcasted_iota(jnp.int32, below.shape, 1) < width
            below = jnp.where(left, 0.0, below) - mm(dot_nn, split(below), split(solved))
            rows[span:] = [below[SUB * i : SUB * (i + 1), :] for i in range(count - span)]
    return jnp.concatenate(out, axis=0)


def invert_panel(at, work, beside=None):
    row = lax.broadcasted_iota(jnp.int32, (BLK, BLK), 0)
    col = lax.broadcasted_iota(jnp.int32, (BLK, BLK), 1)
    lane_block = lax.broadcasted_iota(jnp.int32, (BLK, PANEL), 1) // BLK
    row_block = lax.broadcasted_iota(jnp.int32, (PANEL - BLK, 1), 0) // BLK + 1
    later_block = lax.broadcasted_iota(jnp.int32, (PANEL - BLK, PANEL), 1) // BLK
    one = jnp.full((SUB, BLK), 1.0, F32) * jnp.minimum(at[2], 1).astype(F32)

    def step(b, carry):
        here = pl.ds(pl.multiple_of(b * BLK, BLK), BLK)
        if beside is not None:
            beside(b)
        inv = jnp.where(row >= col, factor_block(work[b, :, here], one), 0.0)
        inv = split(inv) + (inv,)
        across = mm(dot_nn, inv[:2], split(work[b]))
        across = jnp.where(lane_block == b, jnp.concatenate([inv[2]] * NB, axis=1), across)
        across_parts = split(across)
        work[b] = across

        @pl.when(b < NB - 1)
        def _():
            later = work[1:].reshape(PANEL - BLK, PANEL)
            mine = work[1:, :, here].reshape(PANEL - BLK, BLK)
            below = jnp.where(row_block > b, mm(dot_nt, split(mine), inv[:2]), 0.0)
            kept = jnp.where((row_block > b) & (later_block == b), 0.0, later)
            work[1:] = (kept - mm(dot_nn, split(below), across_parts)).reshape(NB - 1, BLK, PANEL)

        return carry

    lax.fori_loop(0, NB, step, 0)


def lower_parts(work, parts, flipped=None):
    lane_block = lax.broadcasted_iota(jnp.int32, (BLK, PANEL), 1) // BLK
    for i in range(NB):
        rows = slice(i * BLK, (i + 1) * BLK)
        lower = jnp.where(lane_block <= i, work[i], 0.0)
        parts[0, rows, :], parts[1, rows, :] = split(lower)
        if flipped is not None:
            for j in range(NB):
                flip = split(lower[:, j * BLK : (j + 1) * BLK].T)
                for p in range(2):
                    flipped[p, j * BLK : (j + 1) * BLK, rows] = flip[p]


def turned(q, j):
    return pl.ds(pl.multiple_of((q + j) % NB * BLK, BLK), BLK)


def take_pivot(at, blocks, work, sem=None):
    core = at[1] % 2

    for chip, own in enumerate(((0, 1), (1, 0), (3, 2), (2, 3))):

        @pl.when(at[1] // 2 == chip)
        def _():
            for i in range(2):
                for k in range(2):
                    source, to = blocks[4 * k + own[i]], work.at[2 * i + (core + k) % 2]
                    if sem is None:
                        for j in range(NB - 1):
                            to[:, turned(2 * i + (core + k) % 2, j)] = source[:, j * BLK : (j + 1) * BLK]
                    else:
                        pltpu.make_async_copy(source, to, sem).start()

    if sem is None:
        for q in range(NB):
            before = (q + NB - 1) % NB
            work[q, :, before * BLK : (before + 1) * BLK] = work[before, :, q * BLK : (q + 1) * BLK].T
    else:
        pltpu.make_async_copy(work, work, sem).wait()


def first_kernel(at, b0, b1, b2, b3, b4, b5, b6, b7, inv_out, work, inv, sem):
    take_pivot(at, (b0, b1, b2, b3, b4, b5, b6, b7), work, sem)
    invert_panel(at, work)
    lower_parts(work, inv.at[0], inv.at[1])
    copy = pltpu.make_async_copy(inv, inv_out, sem)
    copy.start()
    copy.wait()


def pair(ref, rows=slice(None)):
    return ref[0, rows, :], ref[1, rows, :]


def child_kernel(at, mid, own_far, inv0, factor, contribution, own, work, inv1, above, low_first, low_second, rows_second, own_first, sem):
    fetch = pltpu.make_async_copy(own_far.at[:, :, : PC + PANEL], own, sem)
    fetch.start()
    upper = mid[NB:, :, :PANEL].reshape(PANEL, PANEL)
    upper_parts = split(upper)
    solved = split(mm(dot_nt, upper_parts, pair(inv0.at[0])))
    flipped = split(mm(dot_nt, pair(inv0.at[0]), upper_parts))
    above[0], above[1] = flipped
    second = mid[NB:, :, PANEL:].reshape(PANEL, PANEL) - mm(dot_nn, solved, flipped)
    work[...] = second.reshape(NB, BLK, PANEL)
    chunk = 2 * BLK // NB
    fetch.wait()

    def beside(b):
        to = pl.ds(pl.multiple_of(b * BLK, BLK), BLK)
        part = split(mm(dot_nn, split(mid[b, :, :PANEL]), pair(inv0.at[1])))
        low_first[0, to, :], low_first[1, to, :] = part
        rows_second[to, :] = mid[b, :, PANEL:] - mm(dot_nn, part, pair(above))
        s = b // 2
        rows = pl.ds(pl.multiple_of((b % 2) * chunk, chunk), chunk)
        first = mm(dot_nn, split(own[s, rows, :PANEL]), pair(inv0.at[1]))
        factor[s, rows, :PANEL] = first
        part = split(first)
        to = pl.ds(pl.multiple_of(b * chunk, chunk), chunk)
        own_first[0, to, :], own_first[1, to, :] = part
        to = pl.ds(pl.multiple_of(PANEL + b * chunk, chunk), chunk)
        rows_second[to, :] = own[s, rows, PANEL:PC] - mm(dot_nn, part, pair(above))

    invert_panel(at, work, beside)
    lower_parts(work, inv1)
    result = mm(dot_nt, split(rows_second[...]), pair(inv1))
    low_second[0], low_second[1] = split(result[:PANEL])
    second = result[PANEL + BLK :]
    rest = own[1, :, PC : PC + PANEL] - mm(dot_nt, pair(own_first, slice(BLK, None)), pair(low_first))
    rest = (rest - mm(dot_nt, split(second), pair(low_second))).astype(BF16)
    for i in range(TILES):
        r, k = i // NB * TILE, i % NB * BLK
        contribution[i] = rest[r : r + TILE, k : k + BLK]
    factor[0, :, PANEL:] = jnp.where(at[1] < NB, 0.0, result[PANEL : PANEL + BLK])
    factor[1, :, PANEL:] = second


def pack_kernel(at, parent_of, owner_slot, tiles, out, count):
    def clear(s, carry):
        count[s] = 0
        return carry

    def place(c, carry):
        slot = owner_slot[parent_of[c]]
        out[slot, count[slot]] = tiles[c]
        count[slot] = count[slot] + 1
        return carry

    lax.fori_loop(0, out.shape[0], clear, 0, unroll=8)
    lax.fori_loop(0, tiles.shape[0], place, 0, unroll=4)


def assemble_kernel(at, parent_of, owner_slot, front_blocks, block_lists, entries, tiles, out, pivot):
    leaf = at[0]

    def find(q, live):
        return jnp.where(owner_slot[q] == leaf, front_blocks[q], live)

    live = lax.fori_loop(0, owner_slot.shape[0], find, jnp.int32(0))
    for t in range(entries.shape[0]):
        alive = t * at[2] + at[1] < live
        out[t] = jnp.where(alive, entries[t], 0.0)

    def add(c, k):
        hit = owner_slot[parent_of[c]] == leaf

        @pl.when(hit)
        def _():
            t = block_lists[c, at[1]] // at[2]
            for b in range(NB):

                @pl.when(block_lists[c, b] == b)
                def _():
                    for i in range(b, TILES, NB):
                        rows, cols = slice(i // NB * TILE, (i // NB + 1) * TILE), slice(b * BLK, (b + 1) * BLK)
                        out[t, rows, cols] = out[t, rows, cols] + tiles[i, k].astype(F32)

        return k + hit.astype(jnp.int32)

    lax.fori_loop(0, parent_of.shape[0], add, jnp.int32(0))
    for j in range(NB - 1):
        pivot[:, j * BLK : (j + 1) * BLK] = out[0, :, turned(at[1], j)]


def parent_kernel(at, b0, b1, b2, b3, b4, b5, b6, b7, rows, factor, work, inv):
    take_pivot(at, (b0, b1, b2, b3, b4, b5, b6, b7), work)
    invert_panel(at, work)
    lower_parts(work, inv)
    slots = rows.shape[0]
    solved = mm(dot_nt, split(rows[...].reshape(slots * BLK, PANEL)), pair(inv))
    factor[...] = solved.reshape(slots, BLK, PANEL)


VMEM = pl.BlockSpec(memory_space=pltpu.VMEM)
SMEM = pl.BlockSpec(memory_space=pltpu.SMEM)
ANY = pl.BlockSpec(memory_space=pl.ANY)
HBM = pl.BlockSpec(memory_space=pltpu.HBM)


def limit(mib):
    return pltpu.CompilerParams(vmem_limit_bytes=mib * 1024 * 1024)


def shape(*dims, dtype=F32):
    return jax.ShapeDtypeStruct(dims, dtype)


def chip_permute(x, pairs):
    return lax.ppermute(x, "panel", [(2 * a + c, 2 * b + c) for a, b in pairs for c in range(2)])


def gather_pivot(block):
    near = chip_permute(block, ((0, 1), (1, 0)))
    next_ = chip_permute(block, ((0, 3), (1, 2)))
    far = chip_permute(block, ((0, 2), (1, 3)))
    blocks = (block, near, next_, far)
    return blocks + tuple(lax.ppermute(b, "panel", [(i, i ^ 1) for i in range(8)]) for b in blocks)


def add_children(depth, at, tables, entries, tiles):
    parent_of, owner_slot, front_blocks, block_lists = tables
    sends = pl.pallas_call(
        pack_kernel,
        out_shape=shape(TILES, depth, TILE, BLK, dtype=BF16),
        in_specs=[SMEM, SMEM, SMEM, VMEM],
        out_specs=VMEM,
        scratch_shapes=[pltpu.SMEM((TILES,), jnp.int32)],
        compiler_params=limit(8),
        name=f"pack{depth}",
    )(at, parent_of, owner_slot, tiles)
    mine = lax.all_to_all(sends, "leaf", 0, 0, tiled=True)
    return pl.pallas_call(
        assemble_kernel,
        out_shape=(shape(*entries.shape), shape(BLK, PANEL - BLK)),
        in_specs=[SMEM, SMEM, SMEM, SMEM, SMEM, VMEM, VMEM],
        out_specs=(VMEM, VMEM),
        compiler_params=limit(12),
        name=f"assemble{depth}",
    )(at, parent_of, owner_slot, front_blocks, block_lists, entries, mine)


def on_device(child_front, parent_entries, parent_of, owner_slot, front_blocks, block_lists):
    panel_count = lax.axis_size("panel")
    panel = lax.axis_index("panel")
    leaf = lax.axis_index("leaf")
    parent_slots = parent_entries.shape[1]
    own = child_front.reshape(2, BLK, WC)
    with jax.named_scope("mid"):
        slot = (panel < NB).astype(jnp.int32)
        one = lax.dynamic_slice(own, (slot, jnp.int32(0), jnp.int32(0)), (1, BLK, PC))
        mid = lax.all_gather(one, "panel", axis=0, tiled=True)
    with jax.named_scope("pivot0"):
        blocks = gather_pivot(own[0, :, :PANEL])
    at = jnp.stack([leaf, panel, panel_count]).astype(jnp.int32)
    work = pltpu.VMEM((NB, BLK, PANEL), F32)
    parts = pltpu.VMEM((2, PANEL, PANEL), BF16)
    inv0 = pl.pallas_call(
        first_kernel,
        out_shape=shape(2, 2, PANEL, PANEL, dtype=BF16),
        in_specs=[SMEM] + [ANY] * 8,
        out_specs=HBM,
        scratch_shapes=[work, pltpu.VMEM((2, 2, PANEL, PANEL), BF16), pltpu.SemaphoreType.DMA],
        compiler_params=limit(12),
        name="first_panel",
    )(at, *[pltpu.with_memory_space_constraint(b, pltpu.HBM) for b in blocks])
    factor, contribution = pl.pallas_call(
        child_kernel,
        out_shape=(shape(2, BLK, PC), shape(TILES, TILE, BLK, dtype=BF16)),
        in_specs=[SMEM, VMEM, HBM, VMEM],
        out_specs=(VMEM, VMEM),
        scratch_shapes=[
            pltpu.VMEM((2, BLK, PC + PANEL), F32),
            work,
            parts,
            parts,
            parts,
            parts,
            pltpu.VMEM((PANEL + 2 * BLK, PANEL), F32),
            pltpu.VMEM((2, 2 * BLK, PANEL), BF16),
            pltpu.SemaphoreType.DMA,
        ],
        compiler_params=limit(28),
        name="child",
    )(at, mid, pltpu.with_memory_space_constraint(own, pltpu.HBM), inv0)
    slots = jnp.sum(jnp.where(parent_of[:, None] == jnp.arange(owner_slot.shape[0])[None, :], owner_slot[None, :], 0), axis=1)
    most = jnp.max(jnp.sum((slots[:, None] == jnp.arange(TILES)[None, :]).astype(jnp.int32), axis=0))
    with jax.named_scope("tiles"):
        tiles = lax.all_to_all(contribution, "leaf", 0, 0, tiled=True)
    tables = (parent_of, owner_slot, front_blocks, block_lists)
    depths = (4, 6, parent_of.shape[0])
    with jax.named_scope("children"):
        assembled, pivot = lax.switch(
            (most > depths[0]).astype(jnp.int32) + (most > depths[1]).astype(jnp.int32),
            [lambda e, r, d=d: add_children(d, at, tables, e, r) for d in depths],
            parent_entries.reshape(parent_slots, BLK, PANEL),
            tiles,
        )
    with jax.named_scope("pivot2"):
        blocks = gather_pivot(pivot)
    parent_factor = pl.pallas_call(
        parent_kernel,
        out_shape=shape(parent_slots, BLK, PANEL),
        in_specs=[SMEM] + [VMEM] * 9,
        out_specs=VMEM,
        scratch_shapes=[
            work,
            parts,
        ],
        compiler_params=limit(14),
        name="parent",
    )(at, *blocks, assembled)
    return (factor.reshape(child_front.shape[:-1] + (PC,)), parent_factor.reshape(parent_entries.shape))


def solution(mesh):
    front = P("leaf", None, "panel", None, None)
    return jax.shard_map(
        on_device,
        mesh=mesh,
        in_specs=(front, front, P(), P(), P(), P()),
        out_specs=(front, front),
        check_vma=False,
    )
```

```python
import functools

import jax
import jax.numpy as jnp
from jax import lax
from jax.experimental import pallas as pl
from jax.experimental.pallas import tpu as pltpu
from jax.sharding import PartitionSpec as P

BLK = 128
PANEL = 512
WC = 2048
PC = 1024
CBB = 8
NB = PANEL // BLK
SUB = 8
TILE = 16
TILES = BLK // TILE * NB
F32 = jnp.float32
BF16 = jnp.bfloat16


def split(a):
    hi = a.astype(BF16)
    return hi, (a - hi.astype(F32)).astype(BF16)


def dot_nn(a, b):
    return lax.dot_general(a, b, (((1,), (0,)), ((), ())), preferred_element_type=F32)


def dot_nt(a, b):
    return lax.dot_general(a, b, (((1,), (1,)), ((), ())), preferred_element_type=F32)


def mm(dot, a, b):
    (ah, al), (bh, bl) = a, b
    return dot(ah, bh) + (dot(al, bh) + dot(ah, bl))


def lanes(v, j):
    return jnp.broadcast_to(v[:, j : j + 1], (SUB, BLK))


def sublanes(v, k):
    return jnp.broadcast_to(v[k : k + 1, :], (SUB, BLK))


def total(terms):
    while len(terms) > 1:
        terms = [a + b for a, b in zip(terms[::2], terms[1::2])] + terms[len(terms) // 2 * 2 :]
    return terms[0]


def factor_block(block, one):
    count = BLK // SUB
    span = count // 2
    width = span * SUB
    sub = lax.broadcasted_iota(jnp.int32, (SUB, BLK), 0)
    lane = lax.broadcasted_iota(jnp.int32, (SUB, BLK), 1)
    rows = [block[SUB * i : SUB * (i + 1), :] for i in range(count)]
    out = [None] * count
    for half in range(2):
        base = half * span
        now = rows[base : base + span]
        cols = None
        for g in range(span):
            first = SUB * (base + g)
            inside = (lane >= first) & (lane < first + SUB)
            follows = g + 1 < span
            if cols is None:
                cols = [lanes(now[g], first + k) * one for k in range(SUB)]
            if follows:
                kept = [lanes(now[g + 1], first + k) for k in range(SUB)]
                after = [lanes(now[g + 1], first + SUB + k) for k in range(SUB)]
                weights = [w * one for w in kept]
            head = jnp.where(inside, jnp.where(lane == first + sub, 1.0, 0.0), now[g])
            done = jnp.zeros((SUB, BLK), F32)
            for k in range(SUB):
                across = [sublanes(cols[q], k) if q >= k else None for q in range(SUB)]
                inv = 1.0 / across[k]
                here = sub == k
                row = sublanes(head, k)
                for q in range(k + 1, SUB):
                    step = jnp.where(here, -across[q], cols[k] * across[q])
                    cols[q] = jnp.where(here, 0.0, cols[q]) - step * inv
                step = jnp.where(here, -row, cols[k] * row)
                done = jnp.where(here, row * lax.rsqrt(across[k]), done)
                head = jnp.where(here, 0.0, head) - step * inv
                if follows:
                    scaled = weights[k] * inv
                    for q in range(k + 1, SUB):
                        weights[q] = weights[q] - scaled * across[q]
                    for q in range(SUB):
                        after[q] = after[q] - scaled * sublanes(weights[k], q)
            out[base + g] = done
            if base + g == count - 1:
                break
            spread = [sublanes(head, k) for k in range(SUB)]
            others = list(range(g + 1, span)) + (list(range(g)) if half == 0 else [])
            for i in others:
                mult = kept if i == g + 1 else [lanes(now[i], first + k) for k in range(SUB)]
                now[i] = jnp.where(inside, 0.0, now[i]) - total([m * r for m, r in zip(mult, spread)])
            now[g] = head
            cols = after if follows else None
        if half == 0:
            below = jnp.concatenate(rows[span:], axis=0)
            solved = jnp.concatenate(now + [jnp.zeros((BLK - width, BLK), F32)], axis=0)
            left = lax.broadcasted_iota(jnp.int32, below.shape, 1) < width
            below = jnp.where(left, 0.0, below) - mm(dot_nn, split(below), split(solved))
            rows[span:] = [below[SUB * i : SUB * (i + 1), :] for i in range(count - span)]
    return jnp.concatenate(out, axis=0)


def invert_panel(at, work, beside=None):
    row = lax.broadcasted_iota(jnp.int32, (BLK, BLK), 0)
    col = lax.broadcasted_iota(jnp.int32, (BLK, BLK), 1)
    lane_block = lax.broadcasted_iota(jnp.int32, (BLK, PANEL), 1) // BLK
    row_block = lax.broadcasted_iota(jnp.int32, (PANEL - BLK, 1), 0) // BLK + 1
    later_block = lax.broadcasted_iota(jnp.int32, (PANEL - BLK, PANEL), 1) // BLK
    one = jnp.full((SUB, BLK), 1.0, F32) * jnp.minimum(at[2], 1).astype(F32)

    def step(b, carry):
        here = pl.ds(pl.multiple_of(b * BLK, BLK), BLK)
        if beside is not None:
            beside(b)
        inv = jnp.where(row >= col, factor_block(work[b, :, here], one), 0.0)
        inv = split(inv) + (inv,)
        across = mm(dot_nn, inv[:2], split(work[b]))
        across = jnp.where(lane_block == b, jnp.concatenate([inv[2]] * NB, axis=1), across)
        across_parts = split(across)
        work[b] = across

        @pl.when(b < NB - 1)
        def _():
            later = work[1:].reshape(PANEL - BLK, PANEL)
            mine = work[1:, :, here].reshape(PANEL - BLK, BLK)
            below = jnp.where(row_block > b, mm(dot_nt, split(mine), inv[:2]), 0.0)
            kept = jnp.where((row_block > b) & (later_block == b), 0.0, later)
            work[1:] = (kept - mm(dot_nn, split(below), across_parts)).reshape(NB - 1, BLK, PANEL)

        return carry

    lax.fori_loop(0, NB, step, 0)


def lower_parts(work, parts, flipped=None):
    lane_block = lax.broadcasted_iota(jnp.int32, (BLK, PANEL), 1) // BLK
    for i in range(NB):
        rows = slice(i * BLK, (i + 1) * BLK)
        lower = jnp.where(lane_block <= i, work[i], 0.0)
        parts[0, rows, :], parts[1, rows, :] = split(lower)
        if flipped is not None:
            for j in range(NB):
                flip = split(lower[:, j * BLK : (j + 1) * BLK].T)
                for p in range(2):
                    flipped[p, j * BLK : (j + 1) * BLK, rows] = flip[p]


def turned(q, j):
    return pl.ds(pl.multiple_of((q + j) % NB * BLK, BLK), BLK)


def take_pivot(at, blocks, work, sem=None):
    core = at[1] % 2

    for chip, own in enumerate(((0, 1), (1, 0), (3, 2), (2, 3))):

        @pl.when(at[1] // 2 == chip)
        def _():
            for i in range(2):
                for k in range(2):
                    source, to = blocks[4 * k + own[i]], work.at[2 * i + (core + k) % 2]
                    if sem is None:
                        for j in range(NB - 1):
                            to[:, turned(2 * i + (core + k) % 2, j)] = source[:, j * BLK : (j + 1) * BLK]
                    else:
                        pltpu.make_async_copy(source, to, sem).start()

    if sem is None:
        for q in range(NB):
            before = (q + NB - 1) % NB
            work[q, :, before * BLK : (before + 1) * BLK] = work[before, :, q * BLK : (q + 1) * BLK].T
    else:
        pltpu.make_async_copy(work, work, sem).wait()


def first_kernel(at, b0, b1, b2, b3, b4, b5, b6, b7, inv_out, work, inv, sem):
    take_pivot(at, (b0, b1, b2, b3, b4, b5, b6, b7), work, sem)
    invert_panel(at, work)
    lower_parts(work, inv.at[0], inv.at[1])
    copy = pltpu.make_async_copy(inv, inv_out, sem)
    copy.start()
    copy.wait()


def pair(ref, rows=slice(None)):
    return ref[0, rows, :], ref[1, rows, :]


def child_kernel(at, mid_far, own_far, inv0, factor, contribution, mid, own, work, inv1, above, low_first, low_second, rows_second, own_first, sems):
    spans = [(slice(NB, None), slice(0, PANEL)), (slice(NB, None), slice(PANEL, None)), (slice(0, NB), slice(None))]
    fetches = [
        pltpu.make_async_copy(mid_far.at[b, :, c], mid.at[b, :, c], sems.at[i]) for i, (b, c) in enumerate(spans)
    ]
    fetches.append(pltpu.make_async_copy(own_far.at[:, :, : PC + PANEL], own, sems.at[3]))
    for fetch in fetches:
        fetch.start()
    fetches[0].wait()
    upper = mid[NB:, :, :PANEL].reshape(PANEL, PANEL)
    upper_parts = split(upper)
    solved = split(mm(dot_nt, upper_parts, pair(inv0.at[0])))
    flipped = split(mm(dot_nt, pair(inv0.at[0]), upper_parts))
    above[0], above[1] = flipped
    fetches[1].wait()
    second = mid[NB:, :, PANEL:].reshape(PANEL, PANEL) - mm(dot_nn, solved, flipped)
    work[...] = second.reshape(NB, BLK, PANEL)
    chunk = 2 * BLK // NB
    fetches[2].wait()
    fetches[3].wait()

    def beside(b):
        to = pl.ds(pl.multiple_of(b * BLK, BLK), BLK)
        part = split(mm(dot_nn, split(mid[b, :, :PANEL]), pair(inv0.at[1])))
        low_first[0, to, :], low_first[1, to, :] = part
        rows_second[to, :] = mid[b, :, PANEL:] - mm(dot_nn, part, pair(above))
        s = b // 2
        rows = pl.ds(pl.multiple_of((b % 2) * chunk, chunk), chunk)
        first = mm(dot_nn, split(own[s, rows, :PANEL]), pair(inv0.at[1]))
        factor[s, rows, :PANEL] = first
        part = split(first)
        to = pl.ds(pl.multiple_of(b * chunk, chunk), chunk)
        own_first[0, to, :], own_first[1, to, :] = part
        to = pl.ds(pl.multiple_of(PANEL + b * chunk, chunk), chunk)
        rows_second[to, :] = own[s, rows, PANEL:PC] - mm(dot_nn, part, pair(above))

    invert_panel(at, work, beside)
    lower_parts(work, inv1)
    result = mm(dot_nt, split(rows_second[...]), pair(inv1))
    low_second[0], low_second[1] = split(result[:PANEL])
    second = result[PANEL + BLK :]
    rest = own[1, :, PC : PC + PANEL] - mm(dot_nt, pair(own_first, slice(BLK, None)), pair(low_first))
    rest = (rest - mm(dot_nt, split(second), pair(low_second))).astype(BF16)
    for i in range(TILES):
        r, k = i // NB * TILE, i % NB * BLK
        contribution[i] = rest[r : r + TILE, k : k + BLK]
    factor[0, :, PANEL:] = jnp.where(at[1] < NB, 0.0, result[PANEL : PANEL + BLK])
    factor[1, :, PANEL:] = second


def pack_kernel(at, parent_of, owner_slot, tiles, out, count):
    def clear(s, carry):
        count[s] = 0
        return carry

    def place(c, carry):
        slot = owner_slot[parent_of[c]]
        out[slot, count[slot]] = tiles[c]
        count[slot] = count[slot] + 1
        return carry

    lax.fori_loop(0, out.shape[0], clear, 0, unroll=8)
    lax.fori_loop(0, tiles.shape[0], place, 0, unroll=4)


def assemble_kernel(at, parent_of, owner_slot, front_blocks, block_lists, entries, tiles, out, pivot):
    leaf = at[0]

    def find(q, live):
        return jnp.where(owner_slot[q] == leaf, front_blocks[q], live)

    live = lax.fori_loop(0, owner_slot.shape[0], find, jnp.int32(0))
    for t in range(entries.shape[0]):
        alive = t * at[2] + at[1] < live
        out[t] = jnp.where(alive, entries[t], 0.0)

    def add(c, k):
        hit = owner_slot[parent_of[c]] == leaf

        @pl.when(hit)
        def _():
            t = block_lists[c, at[1]] // at[2]
            for b in range(NB):

                @pl.when(block_lists[c, b] == b)
                def _():
                    for i in range(b, TILES, NB):
                        rows, cols = slice(i // NB * TILE, (i // NB + 1) * TILE), slice(b * BLK, (b + 1) * BLK)
                        out[t, rows, cols] = out[t, rows, cols] + tiles[i, k].astype(F32)

        return k + hit.astype(jnp.int32)

    lax.fori_loop(0, parent_of.shape[0], add, jnp.int32(0))
    for j in range(NB - 1):
        pivot[:, j * BLK : (j + 1) * BLK] = out[0, :, turned(at[1], j)]


def parent_kernel(at, b0, b1, b2, b3, b4, b5, b6, b7, rows, factor, work, inv):
    take_pivot(at, (b0, b1, b2, b3, b4, b5, b6, b7), work)
    invert_panel(at, work)
    lower_parts(work, inv)
    slots = rows.shape[0]
    solved = mm(dot_nt, split(rows[...].reshape(slots * BLK, PANEL)), pair(inv))
    factor[...] = solved.reshape(slots, BLK, PANEL)


VMEM = pl.BlockSpec(memory_space=pltpu.VMEM)
SMEM = pl.BlockSpec(memory_space=pltpu.SMEM)
ANY = pl.BlockSpec(memory_space=pl.ANY)
HBM = pl.BlockSpec(memory_space=pltpu.HBM)


def limit(mib):
    return pltpu.CompilerParams(vmem_limit_bytes=mib * 1024 * 1024)


def shape(*dims, dtype=F32):
    return jax.ShapeDtypeStruct(dims, dtype)


def chip_permute(x, pairs):
    return lax.ppermute(x, "panel", [(2 * a + c, 2 * b + c) for a, b in pairs for c in range(2)])


def gather_pivot(block):
    near = chip_permute(block, ((0, 1), (1, 0)))
    next_ = chip_permute(block, ((0, 3), (1, 2)))
    far = chip_permute(block, ((0, 2), (1, 3)))
    blocks = (block, near, next_, far)
    return blocks + tuple(lax.ppermute(b, "panel", [(i, i ^ 1) for i in range(8)]) for b in blocks)


def add_children(depth, at, tables, entries, tiles):
    parent_of, owner_slot, front_blocks, block_lists = tables
    sends = pl.pallas_call(
        pack_kernel,
        out_shape=shape(TILES, depth, TILE, BLK, dtype=BF16),
        in_specs=[SMEM, SMEM, SMEM, VMEM],
        out_specs=VMEM,
        scratch_shapes=[pltpu.SMEM((TILES,), jnp.int32)],
        compiler_params=limit(8),
        name=f"pack{depth}",
    )(at, parent_of, owner_slot, tiles)
    mine = lax.all_to_all(sends, "leaf", 0, 0, tiled=True)
    return pl.pallas_call(
        assemble_kernel,
        out_shape=(shape(*entries.shape), shape(BLK, PANEL - BLK)),
        in_specs=[SMEM, SMEM, SMEM, SMEM, SMEM, VMEM, VMEM],
        out_specs=(VMEM, VMEM),
        compiler_params=limit(12),
        name=f"assemble{depth}",
    )(at, parent_of, owner_slot, front_blocks, block_lists, entries, mine)


def on_device(child_front, parent_entries, parent_of, owner_slot, front_blocks, block_lists):
    panel_count = lax.axis_size("panel")
    panel = lax.axis_index("panel")
    leaf = lax.axis_index("leaf")
    parent_slots = parent_entries.shape[1]
    own = child_front.reshape(2, BLK, WC)
    with jax.named_scope("mid"):
        slot = (panel < NB).astype(jnp.int32)
        one = lax.dynamic_slice(own, (slot, jnp.int32(0), jnp.int32(0)), (1, BLK, PC))
        mid = lax.all_gather(one, "panel", axis=0, tiled=True)
    with jax.named_scope("pivot0"):
        blocks = gather_pivot(own[0, :, :PANEL])
    at = jnp.stack([leaf, panel, panel_count]).astype(jnp.int32)
    work = pltpu.VMEM((NB, BLK, PANEL), F32)
    parts = pltpu.VMEM((2, PANEL, PANEL), BF16)
    inv0 = pl.pallas_call(
        first_kernel,
        out_shape=shape(2, 2, PANEL, PANEL, dtype=BF16),
        in_specs=[SMEM] + [ANY] * 8,
        out_specs=HBM,
        scratch_shapes=[work, pltpu.VMEM((2, 2, PANEL, PANEL), BF16), pltpu.SemaphoreType.DMA],
        compiler_params=limit(12),
        name="first_panel",
    )(at, *[pltpu.with_memory_space_constraint(b, pltpu.HBM) for b in blocks])
    factor, contribution = pl.pallas_call(
        child_kernel,
        out_shape=(shape(2, BLK, PC), shape(TILES, TILE, BLK, dtype=BF16)),
        in_specs=[SMEM, HBM, HBM, VMEM],
        out_specs=(VMEM, VMEM),
        scratch_shapes=[
            pltpu.VMEM((2 * NB, BLK, PC), F32),
            pltpu.VMEM((2, BLK, PC + PANEL), F32),
            work,
            parts,
            parts,
            parts,
            parts,
            pltpu.VMEM((PANEL + 2 * BLK, PANEL), F32),
            pltpu.VMEM((2, 2 * BLK, PANEL), BF16),
            pltpu.SemaphoreType.DMA((4,)),
        ],
        compiler_params=limit(32),
        name="child",
    )(at, pltpu.with_memory_space_constraint(mid, pltpu.HBM), pltpu.with_memory_space_constraint(own, pltpu.HBM), inv0)
    slots = jnp.sum(jnp.where(parent_of[:, None] == jnp.arange(owner_slot.shape[0])[None, :], owner_slot[None, :], 0), axis=1)
    most = jnp.max(jnp.sum((slots[:, None] == jnp.arange(TILES)[None, :]).astype(jnp.int32), axis=0))
    with jax.named_scope("tiles"):
        tiles = lax.all_to_all(contribution, "leaf", 0, 0, tiled=True)
    tables = (parent_of, owner_slot, front_blocks, block_lists)
    depths = (4, 6, parent_of.shape[0])
    with jax.named_scope("children"):
        assembled, pivot = lax.switch(
            (most > depths[0]).astype(jnp.int32) + (most > depths[1]).astype(jnp.int32),
            [lambda e, r, d=d: add_children(d, at, tables, e, r) for d in depths],
            parent_entries.reshape(parent_slots, BLK, PANEL),
            tiles,
        )
    with jax.named_scope("pivot2"):
        blocks = gather_pivot(pivot)
    parent_factor = pl.pallas_call(
        parent_kernel,
        out_shape=shape(parent_slots, BLK, PANEL),
        in_specs=[SMEM] + [VMEM] * 9,
        out_specs=VMEM,
        scratch_shapes=[
            work,
            parts,
        ],
        compiler_params=limit(14),
        name="parent",
    )(at, *blocks, assembled)
    return (factor.reshape(child_front.shape[:-1] + (PC,)), parent_factor.reshape(parent_entries.shape))


def solution(mesh):
    front = P("leaf", None, "panel", None, None)
    return jax.shard_map(
        on_device,
        mesh=mesh,
        in_specs=(front, front, P(), P(), P(), P()),
        out_specs=(front, front),
        check_vma=False,
    )
```
